256 devices in a mesh: dp: 128 (over z, x, y_hi, core), mp: 2 (over y_lo).
Axes of the slice: x: 4, y: 4 (y_hi: 2, y_lo: 2; y = y_hi * 2 + y_lo), z: 8, core: 2. Of those that a mesh axis runs over, the one named last changes fastest.
Arguments:
- features: bfloat16 [16384, 512], P('dp'), may hold values from -6 to 6
- w_in: bfloat16 [512, 512], P(None, 'mp'), may hold values from -0.25 to 0.25
- b_in: float32 [512], P('mp'), may hold values from -1 to 1
- w_out: bfloat16 [512, 128], P('mp'), may hold values from -0.25 to 0.25
- partner: int32 [16384], P('dp'), may hold values from 0 to 16383, as said below
- window: int32 [128], replicated, may hold values from 0 to 3
Outputs:
- row_loss: float32 [4096], P('dp')
- grad_w_in: float32 [512, 512], P(None, 'mp')
- grad_b_in: float32 [512], P('mp')
- grad_w_out: float32 [512, 128], P('mp')
The draws below stay inside these ranges and needn't reach their ends.
Inputs may be any that keep to these rules, and one draw needn't show every extreme that they name: partner pairs the rows: partner[partner[i]] = i and partner[i] != i for every row i.
All inputs are finite; a program needn't handle non-finite values.
Results may differ from the reference program's by a relative error of at most 0.0027.
Values may be sent and summed in bfloat16 or wider, within the bound.
No kernel may reach another device: no remote copies, remote signals or barrier semaphores. Data moves between devices by JAX's collectives and lax.ppermute only.
A program may use at most 64 MiB of HBM per device.

```python
import math
import jax
import jax.numpy as jnp
from jax import lax

C = 512
HID = 512
E = 128
B_DEV = 128
A_DEV = 32
ROWS = 16384
N_DP = 128


def pair_order(key):
    return jax.random.permutation(jax.random.fold_in(key, 7), ROWS).astype(jnp.int32)


def draw_partner(key, part):
    shuffled = pair_order(key)
    swapped = shuffled.reshape(-1, 2)[:, ::-1].reshape(-1)
    return jnp.zeros((ROWS,), jnp.int32).at[shuffled].set(swapped)


def draw_features(key, part):
    shuffled = pair_order(key)
    pair_of = jnp.zeros((ROWS,), jnp.int32).at[shuffled].set(jnp.arange(ROWS, dtype=jnp.int32) // 2)
    pair_count = ROWS // 2
    group_count = max(ROWS // 128, 1)
    member_of = jax.random.randint(jax.random.fold_in(key, 11), (pair_count,), 0, group_count)
    centers = jax.random.normal(jax.random.fold_in(key, 12), (group_count, C), jnp.float32)
    strength = jax.random.uniform(jax.random.fold_in(key, 13), (group_count,), jnp.float32, 0.15, 0.8)
    individual = jax.random.normal(jax.random.fold_in(key, 14), (pair_count, C), jnp.float32)
    jitter = jax.random.normal(jax.random.fold_in(key, 15), (ROWS, C), jnp.float32)
    weight_share = strength[member_of][:, None]
    pair_base = jnp.sqrt(weight_share) * centers[member_of] + jnp.sqrt(1.0 - weight_share) * individual
    crop_views = jnp.sqrt(0.91) * pair_base[pair_of] + 0.3 * jitter
    return jnp.clip(crop_views, -6.0, 6.0).astype(jnp.bfloat16)


def plant(array, stream_key, low, largest):
    shape = array.shape
    index_at = [jax.random.randint(jax.random.fold_in(stream_key, axis), (), 0, shape[axis]) for axis in range(len(shape))]
    array = array.at[tuple(index_at)].set(low)
    longest = shape.index(max(shape))
    index_at[longest] = (index_at[longest] + 1) % shape[longest]
    return array.at[tuple(index_at)].set(largest)


def steps_of(own_key, dims, cuts, smallest, high):
    def one(axis_at, parts):
        draws = jax.random.uniform(jax.random.fold_in(jax.random.fold_in(own_key, 6), axis_at), (parts,), jnp.float32, smallest / len(cuts), high / len(cuts))
        return jnp.repeat(jnp.exp(draws), dims[axis_at] // parts).reshape((-1,) + (1,) * (len(dims) - axis_at - 1))

    factor_of = one(*cuts[0])
    for cut in cuts[1:]:
        factor_of = factor_of * one(*cut)
    return factor_of


def scatter_about(key, dims, deviation, most, split=(), held_as=jnp.bfloat16):
    array = jax.random.normal(key, dims, jnp.float32) * deviation
    if len(split) > 0:
        array = steps_of(key, dims, split, -0.22, 0.18) * array
    return jnp.clip(array, min=-most, max=most).astype(held_as)


def setup_inputs(seed: int = 0) -> dict:
    arg_keys = jax.random.split(jax.random.key(seed), 7)
    features = draw_features(jax.random.fold_in(arg_keys[6], 71), 0)
    w_in = scatter_about(arg_keys[1], (C, HID), C ** -0.5, 0.25, ((1, 2),))
    b_in = jnp.clip(jax.random.uniform(arg_keys[2], (HID,), jnp.float32, -1.0, 1.0) * steps_of(arg_keys[2], (HID,), ((0, 2),), -0.4, 0.0), -1.0, 1.0)
    w_out = scatter_about(arg_keys[3], (HID, E), HID ** -0.5, 0.25, ((0, 2),))
    partner = draw_partner(jax.random.fold_in(arg_keys[6], 71), 0)
    window = plant(jax.random.randint(arg_keys[5], (N_DP,), 0, B_DEV // A_DEV), jax.random.fold_in(arg_keys[5], 1), 0, (B_DEV // A_DEV) - 1).astype(jnp.int32)
    return {"features": features, "w_in": w_in, "b_in": b_in, "w_out": w_out, "partner": partner, "window": window}


INV_TEMP = 10.0
SHIFT = 10.0
EPS = 1e-06

def reference(features, w_in, b_in, w_out, partner, window):
    pre = jnp.dot(features, w_in, preferred_element_type=jnp.float32) + b_in
    hidden = jax.nn.silu(pre).astype(jnp.bfloat16)
    proj = jnp.dot(hidden, w_out, preferred_element_type=jnp.float32)
    norm = jnp.sqrt(lax.optimization_barrier(jnp.sum(proj * proj, axis=1, keepdims=True)) + EPS)
    emb = (proj / norm).astype(jnp.bfloat16)
    total_rows = emb.shape[0]
    width = emb.shape[1]
    shard_count = window.shape[0]
    anchor_idx = ((jnp.arange(shard_count, dtype=jnp.int32) * B_DEV + window.astype(jnp.int32) * A_DEV)[:, None] + jnp.arange(A_DEV, dtype=jnp.int32)[None, :]).reshape(-1).astype(jnp.int32)
    anchor_total = anchor_idx.shape[0]
    anchor_emb = emb[anchor_idx]
    anchor_partner = partner[anchor_idx]
    blk = math.gcd(anchor_total, 512)
    count = anchor_total // blk
    col_ids = jnp.arange(total_rows, dtype=jnp.int32)
    emb_blocks = anchor_emb.reshape(count, blk, width)
    partner_blocks = anchor_partner.reshape(count, blk)
    id_blocks = anchor_idx.reshape(count, blk)

    def stats(carry, item):
        rows_emb, rows_partner, ids = item
        s = jnp.dot(rows_emb, emb.T, preferred_element_type=jnp.float32) * INV_TEMP
        ex = jnp.where(col_ids[None, :] == ids[:, None], 0.0, jnp.exp(s - SHIFT))
        hit = lax.optimization_barrier(jnp.sum(jnp.where(col_ids[None, :] == rows_partner[:, None], s, 0.0), axis=1))
        return (carry, (lax.optimization_barrier(jnp.sum(ex, axis=1)), hit))
    _, (total, hit) = lax.scan(stats, 0, (emb_blocks, partner_blocks, id_blocks))
    total = total.reshape(anchor_total)
    hit = hit.reshape(anchor_total)
    row_loss = jnp.log(total) + SHIFT - hit
    total_blocks = total.reshape(count, blk)

    def grads(acc, item):
        rows_emb, rows_partner, rows_total, ids = item
        s = jnp.dot(rows_emb, emb.T, preferred_element_type=jnp.float32) * INV_TEMP
        prob = jnp.where(col_ids[None, :] == ids[:, None], 0.0, jnp.exp(s - SHIFT) / rows_total[:, None])
        onehot = (col_ids[None, :] == rows_partner[:, None]).astype(jnp.float32)
        weights = (prob - onehot).astype(jnp.bfloat16)
        row_grad = jnp.dot(weights, emb, preferred_element_type=jnp.float32)
        acc = acc + lax.dot_general(weights, rows_emb, (((0,), (0,)), ((), ())), preferred_element_type=jnp.float32)
        return (acc, row_grad)
    col_grad, row_grad = lax.scan(grads, jnp.zeros((total_rows, width), jnp.float32), (emb_blocks, partner_blocks, total_blocks, id_blocks))
    row_full = jnp.zeros((total_rows, width), jnp.float32).at[anchor_idx].add(row_grad.reshape(anchor_total, width))
    grad_emb = (row_full + col_grad) * (INV_TEMP / anchor_total)
    unit = proj / norm
    grad_proj = ((grad_emb - unit * lax.optimization_barrier(jnp.sum(unit * grad_emb, axis=1, keepdims=True))) / norm).astype(jnp.bfloat16)
    grad_w_out = lax.dot_general(hidden, grad_proj, (((0,), (0,)), ((), ())), preferred_element_type=jnp.float32)
    grad_hidden = lax.dot_general(grad_proj, w_out, (((1,), (1,)), ((), ())), preferred_element_type=jnp.float32)
    sig = jax.nn.sigmoid(pre)
    grad_pre = (grad_hidden * sig * (1.0 + pre * (1.0 - sig))).astype(jnp.bfloat16)
    grad_w_in = lax.dot_general(features, grad_pre, (((0,), (0,)), ((), ())), preferred_element_type=jnp.float32)
    grad_b_in = lax.optimization_barrier(jnp.sum(grad_pre.astype(jnp.float32), axis=0))
    return (row_loss, grad_w_in, grad_b_in, grad_w_out)
```

```python
import functools

import jax
import jax.numpy as jnp
from jax import lax
from jax.experimental import pallas as pl
from jax.experimental.pallas import tpu as pltpu
from jax.sharding import Mesh
from jax.sharding import PartitionSpec as P

SIZES = {"z": 8, "x": 4, "yh": 2, "c": 2}
DP = ("z", "x", "yh", "c")
FAR = ("z", "x")
QUAD = ("yh", "c")

ROWS = 128
A_DEV = 32
HALF = 16
EMB = 128
N_FAR = 32
N_QUAD = 4
ANCHORS = N_FAR * HALF
MSG = 24
PART = 88
N_NEAR = 8

INV_TEMP = 10.0
SHIFT = 10.0
EPS = 1e-06
BF16 = jnp.bfloat16
F32 = jnp.float32
I32 = jnp.int32


def call(kernel, outs, *args, smem=(), scratch=()):
    specs = [
        pl.BlockSpec(memory_space=pltpu.SMEM if i in smem else pltpu.VMEM)
        for i in range(len(args))
    ]
    return pl.pallas_call(
        kernel,
        out_shape=[jax.ShapeDtypeStruct(s, d) for s, d in outs],
        in_specs=specs,
        out_specs=[pl.BlockSpec(memory_space=pltpu.VMEM)] * len(outs),
        scratch_shapes=list(scratch),
    )(*args)


def dot(a, b, dims):
    return lax.dot_general(a, b, (dims, ((), ())), preferred_element_type=F32)


def forward(x_ref, w_in_ref, b_ref, w_out_ref, part_ref, pre_ref, hid_ref):
    pre = dot(x_ref[...], w_in_ref[...], ((1,), (0,))) + b_ref[...]
    hidden = (pre * jax.nn.sigmoid(pre)).astype(BF16)
    pre_ref[...] = pre
    hid_ref[...] = hidden
    part_ref[...] = dot(hidden, w_out_ref[...], ((1,), (0,)))


def norm_of(proj):
    return jnp.sqrt(jnp.sum(proj * proj, axis=1, keepdims=True) + EPS)


def embed(at_ref, window_ref, part_ref, other_ref, partner_ref, emb_ref, msg_ref, hold_ref):
    g, q, mp = at_ref[0], at_ref[1], at_ref[2]
    proj = part_ref[...] + other_ref[...]
    emb = (proj / norm_of(proj)).astype(BF16)
    emb_ref[...] = emb
    hold_ref[...] = emb.astype(F32)
    start = pl.multiple_of(window_ref[g * N_QUAD + q] * A_DEV + mp * HALF, HALF)
    chosen = hold_ref[pl.ds(start, HALF), :]
    to = (g % 8) * HALF
    lane = lax.broadcasted_iota(I32, (8, ROWS), 1)
    row = lax.broadcasted_iota(I32, (8, ROWS), 0)
    partner = jnp.broadcast_to(partner_ref[...], (8, ROWS))
    value = jnp.where(
        row == 0, partner // ROWS, jnp.where(row == 1, partner % ROWS, lane)
    ).astype(F32)
    value = pltpu.roll(value, (to - start + ROWS) % ROWS, axis=1)
    value = jnp.where((lane >= to) & (lane < to + HALF) & (row < 3), value, 0.0)
    message = jnp.concatenate([chosen, value], axis=0).astype(BF16)
    for i in range(N_FAR):
        msg_ref[i] = message


def block_ids(at_ref, msg_ref):
    g, q = at_ref[0], at_ref[1]
    ids = msg_ref[:, HALF:, :].astype(F32)
    ids = ids.reshape(N_FAR // 8, 8, 8, ROWS).sum(axis=1)
    ids = jnp.concatenate([ids[i] for i in range(N_FAR // 8)], axis=1)
    lane = lax.broadcasted_iota(I32, (1, ANCHORS), 1)
    partner = (ids[0:1] * float(ROWS) + ids[1:2]).astype(I32)
    own = (lane // HALF * N_QUAD + q) * ROWS + ids[2:3].astype(I32)
    return partner, own


def column_ids(at_ref, r):
    g, q = at_ref[0], at_ref[1]
    base = (g * N_QUAD + (q ^ r)) * ROWS
    return base + lax.broadcasted_iota(I32, (ROWS, 1), 0)


def anchors_of(msg_ref):
    return jnp.concatenate([msg_ref[i, :HALF, :] for i in range(N_FAR)], axis=0)


def totals(at_ref, msg_ref, e0_ref, e1_ref, e2_ref, e3_ref, out_ref):
    anchors = anchors_of(msg_ref)
    partner, own = block_ids(at_ref, msg_ref)
    total = jnp.zeros((1, ANCHORS), F32)
    hit = jnp.zeros((1, ANCHORS), F32)
    for r, e_ref in enumerate((e0_ref, e1_ref, e2_ref, e3_ref)):
        s = dot(e_ref[...], anchors, ((1,), (1,))) * INV_TEMP
        cols = column_ids(at_ref, r)
        ex = jnp.where(cols == own, 0.0, jnp.exp(s - SHIFT))
        total = total + jnp.sum(ex, axis=0, keepdims=True)
        hit = hit + jnp.sum(jnp.where(cols == partner, s, 0.0), axis=0, keepdims=True)
    lines = [total[:, i * ROWS : (i + 1) * ROWS] for i in range(4)]
    lines += [hit[:, i * ROWS : (i + 1) * ROWS] for i in range(4)]
    message = jnp.concatenate(lines, axis=0)
    for i in range(N_FAR):
        out_ref[i] = message


def weights(
    at_ref,
    msg_ref,
    sums_ref,
    e0_ref,
    e1_ref,
    e2_ref,
    e3_ref,
    row_ref,
    c0_ref,
    c1_ref,
    c2_ref,
    c3_ref,
    loss_ref,
):
    anchors = anchors_of(msg_ref)
    partner, own = block_ids(at_ref, msg_ref)
    sums = jnp.sum(sums_ref[...], axis=0)
    total, hit = sums[:4], sums[4:]
    loss_ref[...] = jnp.concatenate([jnp.log(total) + SHIFT - hit, hit], axis=0)
    total = jnp.concatenate([total[i : i + 1] for i in range(4)], axis=1)
    rows = jnp.zeros((ANCHORS, EMB), F32)
    for r, (e_ref, c_ref) in enumerate(
        ((e0_ref, c0_ref), (e1_ref, c1_ref), (e2_ref, c2_ref), (e3_ref, c3_ref))
    ):
        cols_emb = e_ref[...]
        s = dot(cols_emb, anchors, ((1,), (1,))) * INV_TEMP
        cols = column_ids(at_ref, r)
        prob = jnp.where(cols == own, 0.0, jnp.exp(s - SHIFT) / total)
        w = (prob - (cols == partner).astype(F32)).astype(BF16)
        c_ref[...] = dot(w, anchors, ((1,), (0,)))
        rows = rows + dot(w, cols_emb, ((0,), (0,)))
    for i in range(N_FAR):
        row_ref[i] = rows[i * HALF : (i + 1) * HALF]


def gather_rows(
    at_ref, window_ref, rows_ref, c0_ref, r1_ref, r2_ref, r3_ref, loss_ref, out_ref
):
    g, q, mp = at_ref[0], at_ref[1], at_ref[2]
    out_ref[0:ROWS, :] = (c0_ref[...] + r1_ref[...]) + (r2_ref[...] + r3_ref[...])
    start = pl.multiple_of(window_ref[g * N_QUAD + q] * A_DEV + mp * HALF, HALF)
    mine = jnp.sum(rows_ref[...], axis=0)
    out_ref[pl.ds(start, HALF), :] = out_ref[pl.ds(start, HALF), :] + mine
    row = lax.broadcasted_iota(I32, (8, ROWS), 0)
    line = jnp.sum(jnp.where(row == g // 8, loss_ref[...], 0.0), axis=0, keepdims=True)
    line = jnp.broadcast_to(line, (8, ROWS))
    line = pltpu.roll(line, (mp * HALF - (g % 8) * HALF + ROWS) % ROWS, axis=1)
    lane = lax.broadcasted_iota(I32, (8, ROWS), 1)
    out_ref[ROWS:, :] = jnp.where((lane >= mp * HALF) & (lane < mp * HALF + HALF), line, 0.0)


def backward(
    at_ref,
    mine_ref,
    theirs_ref,
    part_ref,
    other_ref,
    pre_ref,
    hid_ref,
    x_ref,
    w_out_ref,
    loss_ref,
    keep_ref,
    send_ref,
    all_ref,
):
    scale = INV_TEMP / (N_FAR * N_QUAD * A_DEV)
    grad_emb = (mine_ref[0:ROWS, :] + theirs_ref[0:ROWS, :]) * scale
    loss_ref[...] = mine_ref[ROWS : ROWS + 1, 0:A_DEV] + theirs_ref[ROWS : ROWS + 1, 0:A_DEV]
    proj = part_ref[...] + other_ref[...]
    norm = norm_of(proj)
    unit = proj / norm
    inner = jnp.sum(unit * grad_emb, axis=1, keepdims=True)
    grad_proj = ((grad_emb - unit * inner) / norm).astype(BF16)
    all_ref[1024:1280, :] = dot(hid_ref[...], grad_proj, ((0,), (0,)))
    grad_hidden = dot(grad_proj, w_out_ref[...], ((1,), (1,)))
    pre = pre_ref[...]
    sig = jax.nn.sigmoid(pre)
    grad_pre = (grad_hidden * sig * (1.0 + pre * (1.0 - sig))).astype(BF16)
    grad_in = dot(x_ref[...], grad_pre, ((0,), (0,)))
    all_ref[0:512, :] = grad_in[:, :128]
    all_ref[512:1024, :] = grad_in[:, 128:]
    bias = jnp.sum(grad_pre.astype(F32), axis=0, keepdims=True)
    bias = jnp.concatenate([bias[:, :128], bias[:, 128:], jnp.zeros((6, 128), F32)], axis=0)
    c = at_ref[1] % 2
    for side, out_ref in ((c, keep_ref), (1 - c, send_ref)):
        base = pl.multiple_of(side * 640, 128)
        for i in range(N_NEAR):
            out_ref[i, 0:80, :] = all_ref[pl.ds(base + i * 80, 80), :]
            out_ref[i, 80:, :] = bias if i == 0 else jnp.zeros((8, 128), F32)


def add(a_ref, b_ref, out_ref):
    out_ref[...] = a_ref[...] + b_ref[...]


def sum_spread(in_ref, out_ref):
    total = jnp.sum(in_ref[...], axis=0)
    for i in range(N_NEAR):
        out_ref[i] = total


def unpack(at_ref, mine_ref, theirs_ref, w_in_ref, b_ref, w_out_ref, all_ref):
    c = at_ref[1] % 2
    for side, in_ref in ((c, mine_ref), (1 - c, theirs_ref)):
        base = pl.multiple_of(side * 640, 128)
        for i in range(N_NEAR):
            all_ref[pl.ds(base + i * 80, 80), :] = in_ref[i, 0:80, :]
    w_in_ref[:, :128] = all_ref[0:512, :]
    w_in_ref[:, 128:] = all_ref[512:1024, :]
    w_out_ref[...] = all_ref[1024:1280, :]
    b_ref[...] = mine_ref[0, 80:82, :]


def swap(value, axes, flip):
    axes = axes if isinstance(axes, tuple) else (axes,)
    count = lax.axis_size(axes)
    return lax.ppermute(value, axes, [(i, i ^ flip) for i in range(count)])


def exchange(value, axes):
    return lax.all_to_all(value, axes, 0, 0, tiled=True)


def on_device(features, w_in, b_in, w_out, partner, window):
    at = jnp.stack([lax.axis_index(FAR), lax.axis_index(QUAD), lax.axis_index("mp")]).astype(I32)
    part, pre, hidden = call(
        forward,
        [((ROWS, EMB), F32), ((ROWS, 256), F32), ((ROWS, 256), BF16)],
        features,
        w_in,
        b_in.reshape(1, -1),
        w_out,
    )
    other = swap(part, "mp", 1)
    emb, message = call(
        embed,
        [((ROWS, EMB), BF16), ((N_FAR, MSG, EMB), BF16)],
        at,
        window,
        part,
        other,
        partner.reshape(1, -1),
        smem=(0, 1),
        scratch=[pltpu.VMEM((ROWS, EMB), F32)],
    )
    anchors = exchange(message, FAR)
    blocks = [emb] + [swap(emb, QUAD, r) for r in (1, 2, 3)]
    (sums,) = call(totals, [((N_FAR, 8, ROWS), F32)], at, anchors, *blocks, smem=(0,))
    sums = exchange(sums, FAR)
    rows, c0, c1, c2, c3, losses = call(
        weights,
        [((N_FAR, HALF, EMB), F32)] + [((ROWS, EMB), F32)] * 4 + [((8, ROWS), F32)],
        at,
        anchors,
        sums,
        *blocks,
        smem=(0,),
    )
    rows = exchange(rows, FAR)
    r1, r2, r3 = [swap(c, QUAD, r) for r, c in ((1, c1), (2, c2), (3, c3))]
    (mine,) = call(
        gather_rows,
        [((ROWS + 8, EMB), F32)],
        at,
        window,
        rows,
        c0,
        r1,
        r2,
        r3,
        losses,
        smem=(0, 1),
    )
    theirs = swap(mine, "mp", 1)
    half = (N_NEAR, PART, EMB)
    row_loss, keep, send = call(
        backward,
        [((1, A_DEV), F32), (half, F32), (half, F32)],
        at,
        mine,
        theirs,
        part,
        other,
        pre,
        hidden,
        features,
        w_out,
        smem=(0,),
        scratch=[pltpu.VMEM((1280, EMB), F32)],
    )
    got = swap(send, "c", 1)
    (both,) = call(add, [(half, F32)], keep, got)
    (both,) = call(sum_spread, [(half, F32)], exchange(both, ("x", "yh")))
    (both,) = call(sum_spread, [(half, F32)], exchange(both, "z"))
    both = exchange(both, ("x", "yh"))
    got = swap(both, "c", 1)
    grad_in, grad_b, grad_out = call(
        unpack,
        [((512, 256), F32), ((2, 128), F32), ((256, EMB), F32)],
        at,
        both,
        got,
        smem=(0,),
        scratch=[pltpu.VMEM((1280, EMB), F32)],
    )
    return (row_loss.reshape(-1), grad_in, grad_b.reshape(-1), grad_out)


def solution(mesh):
    finer = Mesh(mesh.devices.reshape(*SIZES.values(), mesh.shape["mp"]), (*SIZES, "mp"))
    placed = (P(DP, None), P(None, "mp"), P("mp"), P("mp", None), P(DP), P())
    return jax.shard_map(
        on_device,
        mesh=finer,
        in_specs=placed,
        out_specs=(P(DP), P(None, "mp"), P("mp"), P("mp", None)),
        check_vma=False,
    )
```

```python
import functools

import jax
import jax.numpy as jnp
from jax import lax
from jax.experimental import pallas as pl
from jax.experimental.pallas import tpu as pltpu
from jax.sharding import Mesh
from jax.sharding import PartitionSpec as P

SIZES = {"z": 8, "x": 4, "yh": 2, "c": 2}
DP = ("z", "x", "yh", "c")
FAR = ("z", "x")
QUAD = ("yh", "c")

ROWS = 128
A_DEV = 32
HALF = 16
EMB = 128
N_FAR = 32
N_QUAD = 4
ANCHORS = N_FAR * HALF
MSG = 24
PART = 88
N_NEAR = 8

INV_TEMP = 10.0
SHIFT = 10.0
EPS = 1e-06
BF16 = jnp.bfloat16
F32 = jnp.float32
I32 = jnp.int32


def call(kernel, outs, *args, smem=(), scratch=(), first=False, last=False):
    specs = [
        pl.BlockSpec(memory_space=pltpu.SMEM if i in smem else pltpu.VMEM)
        for i in range(len(args))
    ]
    if not first:
        args = [
            a if i in smem else pltpu.with_memory_space_constraint(a, pltpu.VMEM)
            for i, a in enumerate(args)
        ]
    kind = jax.ShapeDtypeStruct if last else pltpu.VMEM
    return pl.pallas_call(
        kernel,
        out_shape=[kind(s, d) for s, d in outs],
        in_specs=specs,
        out_specs=[pl.BlockSpec(memory_space=pltpu.VMEM)] * len(outs),
        scratch_shapes=list(scratch),
    )(*args)


def dot(a, b, dims):
    return lax.dot_general(a, b, (dims, ((), ())), preferred_element_type=F32)


def forward(x_ref, w_in_ref, b_ref, w_out_ref, part_ref, pre_ref, hid_ref):
    pre = dot(x_ref[...], w_in_ref[...], ((1,), (0,))) + b_ref[...]
    hidden = (pre * jax.nn.sigmoid(pre)).astype(BF16)
    pre_ref[...] = pre
    hid_ref[...] = hidden
    part_ref[...] = dot(hidden, w_out_ref[...], ((1,), (0,)))


def norm_of(proj):
    return jnp.sqrt(jnp.sum(proj * proj, axis=1, keepdims=True) + EPS)


def embed(at_ref, window_ref, part_ref, other_ref, partner_ref, emb_ref, msg_ref, hold_ref):
    g, q, mp = at_ref[0], at_ref[1], at_ref[2]
    proj = part_ref[...] + other_ref[...]
    emb = (proj / norm_of(proj)).astype(BF16)
    emb_ref[...] = emb
    hold_ref[...] = emb.astype(F32)
    start = pl.multiple_of(window_ref[g * N_QUAD + q] * A_DEV + mp * HALF, HALF)
    chosen = hold_ref[pl.ds(start, HALF), :]
    to = (g % 8) * HALF
    lane = lax.broadcasted_iota(I32, (8, ROWS), 1)
    row = lax.broadcasted_iota(I32, (8, ROWS), 0)
    partner = jnp.broadcast_to(partner_ref[...], (8, ROWS))
    value = jnp.where(
        row == 0, partner // ROWS, jnp.where(row == 1, partner % ROWS, lane)
    ).astype(F32)
    value = pltpu.roll(value, (to - start + ROWS) % ROWS, axis=1)
    value = jnp.where((lane >= to) & (lane < to + HALF) & (row < 3), value, 0.0)
    message = jnp.concatenate([chosen, value], axis=0).astype(BF16)
    for i in range(N_FAR):
        msg_ref[i] = message


def block_ids(at_ref, msg_ref):
    g, q = at_ref[0], at_ref[1]
    ids = msg_ref[:, HALF:, :].astype(F32)
    ids = ids.reshape(N_FAR // 8, 8, 8, ROWS).sum(axis=1)
    ids = jnp.concatenate([ids[i] for i in range(N_FAR // 8)], axis=1)
    lane = lax.broadcasted_iota(I32, (1, ANCHORS), 1)
    partner = (ids[0:1] * float(ROWS) + ids[1:2]).astype(I32)
    own = (lane // HALF * N_QUAD + q) * ROWS + ids[2:3].astype(I32)
    return partner, own


def column_ids(at_ref, r):
    g, q = at_ref[0], at_ref[1]
    base = (g * N_QUAD + (q ^ r)) * ROWS
    return base + lax.broadcasted_iota(I32, (ROWS, 1), 0)


def anchors_of(msg_ref):
    return jnp.concatenate([msg_ref[i, :HALF, :] for i in range(N_FAR)], axis=0)


def totals(at_ref, msg_ref, e0_ref, e1_ref, e2_ref, e3_ref, out_ref):
    anchors = anchors_of(msg_ref)
    partner, own = block_ids(at_ref, msg_ref)
    total = jnp.zeros((1, ANCHORS), F32)
    hit = jnp.zeros((1, ANCHORS), F32)
    for r, e_ref in enumerate((e0_ref, e1_ref, e2_ref, e3_ref)):
        s = dot(e_ref[...], anchors, ((1,), (1,))) * INV_TEMP
        cols = column_ids(at_ref, r)
        ex = jnp.where(cols == own, 0.0, jnp.exp(s - SHIFT))
        total = total + jnp.sum(ex, axis=0, keepdims=True)
        hit = hit + jnp.sum(jnp.where(cols == partner, s, 0.0), axis=0, keepdims=True)
    lines = [total[:, i * ROWS : (i + 1) * ROWS] for i in range(4)]
    lines += [hit[:, i * ROWS : (i + 1) * ROWS] for i in range(4)]
    message = jnp.concatenate(lines, axis=0)
    for i in range(N_FAR):
        out_ref[i] = message


def weights(
    at_ref,
    msg_ref,
    sums_ref,
    e0_ref,
    e1_ref,
    e2_ref,
    e3_ref,
    row_ref,
    c0_ref,
    c1_ref,
    c2_ref,
    c3_ref,
    loss_ref,
):
    anchors = anchors_of(msg_ref)
    partner, own = block_ids(at_ref, msg_ref)
    sums = jnp.sum(sums_ref[...], axis=0)
    total, hit = sums[:4], sums[4:]
    loss_ref[...] = jnp.concatenate([jnp.log(total) + SHIFT - hit, hit], axis=0)
    total = jnp.concatenate([total[i : i + 1] for i in range(4)], axis=1)
    rows = jnp.zeros((ANCHORS, EMB), F32)
    for r, (e_ref, c_ref) in enumerate(
        ((e0_ref, c0_ref), (e1_ref, c1_ref), (e2_ref, c2_ref), (e3_ref, c3_ref))
    ):
        cols_emb = e_ref[...]
        s = dot(cols_emb, anchors, ((1,), (1,))) * INV_TEMP
        cols = column_ids(at_ref, r)
        prob = jnp.where(cols == own, 0.0, jnp.exp(s - SHIFT) / total)
        w = (prob - (cols == partner).astype(F32)).astype(BF16)
        c_ref[...] = dot(w, anchors, ((1,), (0,)))
        rows = rows + dot(w, cols_emb, ((0,), (0,)))
    for i in range(N_FAR):
        row_ref[i] = rows[i * HALF : (i + 1) * HALF]


def gather_rows(
    at_ref, window_ref, rows_ref, c0_ref, r1_ref, r2_ref, r3_ref, loss_ref, out_ref
):
    g, q, mp = at_ref[0], at_ref[1], at_ref[2]
    out_ref[0:ROWS, :] = (c0_ref[...] + r1_ref[...]) + (r2_ref[...] + r3_ref[...])
    start = pl.multiple_of(window_ref[g * N_QUAD + q] * A_DEV + mp * HALF, HALF)
    mine = jnp.sum(rows_ref[...], axis=0)
    out_ref[pl.ds(start, HALF), :] = out_ref[pl.ds(start, HALF), :] + mine
    row = lax.broadcasted_iota(I32, (8, ROWS), 0)
    line = jnp.sum(jnp.where(row == g // 8, loss_ref[...], 0.0), axis=0, keepdims=True)
    line = jnp.broadcast_to(line, (8, ROWS))
    line = pltpu.roll(line, (mp * HALF - (g % 8) * HALF + ROWS) % ROWS, axis=1)
    lane = lax.broadcasted_iota(I32, (8, ROWS), 1)
    out_ref[ROWS:, :] = jnp.where((lane >= mp * HALF) & (lane < mp * HALF + HALF), line, 0.0)


def backward(
    at_ref,
    mine_ref,
    theirs_ref,
    part_ref,
    other_ref,
    pre_ref,
    hid_ref,
    x_ref,
    w_out_ref,
    loss_ref,
    keep_ref,
    send_ref,
    all_ref,
):
    scale = INV_TEMP / (N_FAR * N_QUAD * A_DEV)
    grad_emb = (mine_ref[0:ROWS, :] + theirs_ref[0:ROWS, :]) * scale
    loss_ref[...] = mine_ref[ROWS : ROWS + 1, 0:A_DEV] + theirs_ref[ROWS : ROWS + 1, 0:A_DEV]
    proj = part_ref[...] + other_ref[...]
    norm = norm_of(proj)
    unit = proj / norm
    inner = jnp.sum(unit * grad_emb, axis=1, keepdims=True)
    grad_proj = ((grad_emb - unit * inner) / norm).astype(BF16)
    all_ref[1024:1280, :] = dot(hid_ref[...], grad_proj, ((0,), (0,)))
    grad_hidden = dot(grad_proj, w_out_ref[...], ((1,), (1,)))
    pre = pre_ref[...]
    sig = jax.nn.sigmoid(pre)
    grad_pre = (grad_hidden * sig * (1.0 + pre * (1.0 - sig))).astype(BF16)
    grad_in = dot(x_ref[...], grad_pre, ((0,), (0,)))
    all_ref[0:512, :] = grad_in[:, :128]
    all_ref[512:1024, :] = grad_in[:, 128:]
    bias = jnp.sum(grad_pre.astype(F32), axis=0, keepdims=True)
    bias = jnp.concatenate([bias[:, :128], bias[:, 128:], jnp.zeros((6, 128), F32)], axis=0)
    c = at_ref[1] % 2
    for side, out_ref in ((c, keep_ref), (1 - c, send_ref)):
        base = pl.multiple_of(side * 640, 128)
        for i in range(N_NEAR):
            out_ref[i, 0:80, :] = all_ref[pl.ds(base + i * 80, 80), :]
            out_ref[i, 80:, :] = bias if i == 0 else jnp.zeros((8, 128), F32)


def add(a_ref, b_ref, out_ref):
    out_ref[...] = a_ref[...] + b_ref[...]


def sum_spread(in_ref, out_ref):
    total = jnp.sum(in_ref[...], axis=0)
    for i in range(N_NEAR):
        out_ref[i] = total


def unpack(at_ref, mine_ref, theirs_ref, w_in_ref, b_ref, w_out_ref, all_ref):
    c = at_ref[1] % 2
    for side, in_ref in ((c, mine_ref), (1 - c, theirs_ref)):
        base = pl.multiple_of(side * 640, 128)
        for i in range(N_NEAR):
            all_ref[pl.ds(base + i * 80, 80), :] = in_ref[i, 0:80, :]
    w_in_ref[:, :128] = all_ref[0:512, :]
    w_in_ref[:, 128:] = all_ref[512:1024, :]
    w_out_ref[...] = all_ref[1024:1280, :]
    b_ref[...] = mine_ref[0, 80:82, :]


def swap(value, axes, flip):
    axes = axes if isinstance(axes, tuple) else (axes,)
    count = lax.axis_size(axes)
    return lax.ppermute(value, axes, [(i, i ^ flip) for i in range(count)])


def exchange(value, axes):
    return lax.all_to_all(value, axes, 0, 0, tiled=True)


def on_device(features, w_in, b_in, w_out, partner, window):
    at = jnp.stack([lax.axis_index(FAR), lax.axis_index(QUAD), lax.axis_index("mp")]).astype(I32)
    part, pre, hidden = call(
        forward,
        [((ROWS, EMB), F32), ((ROWS, 256), F32), ((ROWS, 256), BF16)],
        features,
        w_in,
        b_in.reshape(1, -1),
        w_out,
        first=True,
    )
    other = swap(part, "mp", 1)
    emb, message = call(
        embed,
        [((ROWS, EMB), BF16), ((N_FAR, MSG, EMB), BF16)],
        at,
        window,
        part,
        other,
        partner.reshape(1, -1),
        smem=(0, 1),
        scratch=[pltpu.VMEM((ROWS, EMB), F32)],
    )
    anchors = exchange(message, FAR)
    blocks = [emb] + [swap(emb, QUAD, r) for r in (1, 2, 3)]
    (sums,) = call(totals, [((N_FAR, 8, ROWS), F32)], at, anchors, *blocks, smem=(0,))
    sums = exchange(sums, FAR)
    rows, c0, c1, c2, c3, losses = call(
        weights,
        [((N_FAR, HALF, EMB), F32)] + [((ROWS, EMB), F32)] * 4 + [((8, ROWS), F32)],
        at,
        anchors,
        sums,
        *blocks,
        smem=(0,),
    )
    rows = exchange(rows, FAR)
    r1, r2, r3 = [swap(c, QUAD, r) for r, c in ((1, c1), (2, c2), (3, c3))]
    (mine,) = call(
        gather_rows,
        [((ROWS + 8, EMB), F32)],
        at,
        window,
        rows,
        c0,
        r1,
        r2,
        r3,
        losses,
        smem=(0, 1),
    )
    theirs = swap(mine, "mp", 1)
    half = (N_NEAR, PART, EMB)
    row_loss, keep, send = call(
        backward,
        [((1, A_DEV), F32), (half, F32), (half, F32)],
        at,
        mine,
        theirs,
        part,
        other,
        pre,
        hidden,
        features,
        w_out,
        smem=(0,),
        scratch=[pltpu.VMEM((1280, EMB), F32)],
    )
    got = swap(send, "c", 1)
    (both,) = call(add, [(half, F32)], keep, got)
    (both,) = call(sum_spread, [(half, F32)], exchange(both, ("x", "yh")))
    (both,) = call(sum_spread, [(half, F32)], exchange(both, "z"))
    both = exchange(both, ("x", "yh"))
    got = swap(both, "c", 1)
    grad_in, grad_b, grad_out = call(
        unpack,
        [((512, 256), F32), ((2, 128), F32), ((256, EMB), F32)],
        at,
        both,
        got,
        smem=(0,),
        scratch=[pltpu.VMEM((1280, EMB), F32)],
        last=True,
    )
    return (row_loss.reshape(-1), grad_in, grad_b.reshape(-1), grad_out)


def solution(mesh):
    finer = Mesh(mesh.devices.reshape(*SIZES.values(), mesh.shape["mp"]), (*SIZES, "mp"))
    placed = (P(DP, None), P(None, "mp"), P("mp"), P("mp", None), P(DP), P())
    return jax.shard_map(
        on_device,
        mesh=finer,
        in_specs=placed,
        out_specs=(P(DP), P(None, "mp"), P("mp"), P("mp", None)),
        check_vma=False,
    )
```

```python
import jax
import jax.numpy as jnp
from jax import lax
from jax.experimental import pallas as pl
from jax.experimental.pallas import tpu as pltpu
from jax.sharding import Mesh
from jax.sharding import PartitionSpec as P

SIZES = {"zh": 4, "zl": 2, "x": 4, "yh": 2, "c": 2}
DP = ("zh", "zl", "x", "yh", "c")
NEAR = ("zl", "x", "yh")
FAR = ("zh", "zl", "x")
QUAD = ("yh", "c")

ROWS = 128
A_DEV = 32
HALF = 16
EMB = 128
N_FAR = 32
N_QUAD = 4
ANCHORS = N_FAR * HALF
MSG = 24
PART = 48
N_NEAR = 16

INV_TEMP = 10.0
SHIFT = 10.0
EPS = 1e-06
BF16 = jnp.bfloat16
F32 = jnp.float32
I32 = jnp.int32


def call(kernel, outs, *args, smem=(), scratch=(), first=False, last=(), alias={}):
    specs = [
        pl.BlockSpec(memory_space=pltpu.SMEM if i in smem else pl.ANY if i in alias else pltpu.VMEM)
        for i in range(len(args))
    ]
    if not first:
        args = [
            a if i in smem or i in alias else pltpu.with_memory_space_constraint(a, pltpu.VMEM)
            for i, a in enumerate(args)
        ]
    shapes = [
        jax.ShapeDtypeStruct(s, d) if last else pltpu.VMEM(s, d) for i, (s, d) in enumerate(outs)
    ]
    return pl.pallas_call(
        kernel,
        out_shape=shapes,
        in_specs=specs,
        out_specs=[
            pl.BlockSpec(memory_space=pl.ANY if i in last else pltpu.VMEM) for i in range(len(outs))
        ],
        scratch_shapes=list(scratch),
        input_output_aliases=alias,
    )(*args)


def dot(a, b, dims):
    return lax.dot_general(a, b, (dims, ((), ())), preferred_element_type=F32)


def forward(x_ref, w_in_ref, b_ref, w_out_ref, part_ref, pre_ref, hid_ref):
    pre = dot(x_ref[...], w_in_ref[...], ((1,), (0,))) + b_ref[...]
    hidden = (pre * jax.nn.sigmoid(pre)).astype(BF16)
    pre_ref[...] = pre
    hid_ref[...] = hidden
    part_ref[...] = dot(hidden, w_out_ref[...], ((1,), (0,)))


def norm_of(proj):
    return jnp.sqrt(jnp.sum(proj * proj, axis=1, keepdims=True) + EPS)


def embed(at_ref, window_ref, part_ref, other_ref, partner_ref, emb_ref, msg_ref, hold_ref):
    g, q, mp = at_ref[0], at_ref[1], at_ref[2]
    proj = part_ref[...] + other_ref[...]
    emb = (proj / norm_of(proj)).astype(BF16)
    emb_ref[...] = emb
    hold_ref[...] = emb.astype(F32)
    start = pl.multiple_of(window_ref[g * N_QUAD + q] * A_DEV + mp * HALF, HALF)
    chosen = hold_ref[pl.ds(start, HALF), :]
    to = (g % 8) * HALF
    lane = lax.broadcasted_iota(I32, (8, ROWS), 1)
    row = lax.broadcasted_iota(I32, (8, ROWS), 0)
    partner = jnp.broadcast_to(partner_ref[...], (8, ROWS))
    value = jnp.where(
        row == 0, partner // ROWS, jnp.where(row == 1, partner % ROWS, lane)
    ).astype(F32)
    value = pltpu.roll(value, (to - start + ROWS) % ROWS, axis=1)
    value = jnp.where((lane >= to) & (lane < to + HALF) & (row < 3), value, 0.0)
    message = jnp.concatenate([chosen, value], axis=0).astype(BF16)
    for i in range(N_FAR):
        msg_ref[i] = message


def block_ids(at_ref, msg_ref):
    g, q = at_ref[0], at_ref[1]
    ids = msg_ref[:, HALF:, :].astype(F32)
    ids = ids.reshape(N_FAR // 8, 8, 8, ROWS).sum(axis=1)
    ids = jnp.concatenate([ids[i] for i in range(N_FAR // 8)], axis=1)
    lane = lax.broadcasted_iota(I32, (1, ANCHORS), 1)
    partner = (ids[0:1] * float(ROWS) + ids[1:2]).astype(I32)
    own = (lane // HALF * N_QUAD + q) * ROWS + ids[2:3].astype(I32)
    return partner, own


def column_ids(at_ref, r):
    g, q = at_ref[0], at_ref[1]
    base = (g * N_QUAD + (q ^ r)) * ROWS
    return base + lax.broadcasted_iota(I32, (ROWS, 1), 0)


def anchors_of(msg_ref):
    return jnp.concatenate([msg_ref[i, :HALF, :] for i in range(N_FAR)], axis=0)


def totals(at_ref, msg_ref, e0_ref, e1_ref, e2_ref, e3_ref, out_ref):
    anchors = anchors_of(msg_ref)
    partner, own = block_ids(at_ref, msg_ref)
    total = jnp.zeros((1, ANCHORS), F32)
    hit = jnp.zeros((1, ANCHORS), F32)
    for r, e_ref in enumerate((e0_ref, e1_ref, e2_ref, e3_ref)):
        s = dot(e_ref[...], anchors, ((1,), (1,))) * INV_TEMP
        cols = column_ids(at_ref, r)
        ex = jnp.where(cols == own, 0.0, jnp.exp(s - SHIFT))
        total = total + jnp.sum(ex, axis=0, keepdims=True)
        hit = hit + jnp.sum(jnp.where(cols == partner, s, 0.0), axis=0, keepdims=True)
    lines = [total[:, i * ROWS : (i + 1) * ROWS] for i in range(4)]
    lines += [hit[:, i * ROWS : (i + 1) * ROWS] for i in range(4)]
    message = jnp.concatenate(lines, axis=0)
    for i in range(N_FAR):
        out_ref[i] = message


def weights(
    at_ref,
    msg_ref,
    sums_ref,
    e0_ref,
    e1_ref,
    e2_ref,
    e3_ref,
    row_ref,
    c0_ref,
    c1_ref,
    c2_ref,
    c3_ref,
    loss_ref,
):
    anchors = anchors_of(msg_ref)
    partner, own = block_ids(at_ref, msg_ref)
    sums = jnp.sum(sums_ref[...], axis=0)
    total, hit = sums[:4], sums[4:]
    loss_ref[...] = jnp.concatenate([jnp.log(total) + SHIFT - hit, hit], axis=0)
    total = jnp.concatenate([total[i : i + 1] for i in range(4)], axis=1)
    rows = jnp.zeros((ANCHORS, EMB), F32)
    for r, (e_ref, c_ref) in enumerate(
        ((e0_ref, c0_ref), (e1_ref, c1_ref), (e2_ref, c2_ref), (e3_ref, c3_ref))
    ):
        cols_emb = e_ref[...]
        s = dot(cols_emb, anchors, ((1,), (1,))) * INV_TEMP
        cols = column_ids(at_ref, r)
        prob = jnp.where(cols == own, 0.0, jnp.exp(s - SHIFT) / total)
        w = (prob - (cols == partner).astype(F32)).astype(BF16)
        c_ref[...] = dot(w, anchors, ((1,), (0,)))
        rows = rows + dot(w, cols_emb, ((0,), (0,)))
    for i in range(N_FAR):
        row_ref[i] = rows[i * HALF : (i + 1) * HALF]


def gather_rows(
    at_ref, window_ref, rows_ref, c0_ref, r1_ref, r2_ref, r3_ref, loss_ref, out_ref
):
    g, q, mp = at_ref[0], at_ref[1], at_ref[2]
    out_ref[0:ROWS, :] = (c0_ref[...] + r1_ref[...]) + (r2_ref[...] + r3_ref[...])
    start = pl.multiple_of(window_ref[g * N_QUAD + q] * A_DEV + mp * HALF, HALF)
    mine = jnp.sum(rows_ref[...], axis=0)
    out_ref[pl.ds(start, HALF), :] = out_ref[pl.ds(start, HALF), :] + mine
    row = lax.broadcasted_iota(I32, (8, ROWS), 0)
    line = jnp.sum(jnp.where(row == g // 8, loss_ref[...], 0.0), axis=0, keepdims=True)
    line = jnp.broadcast_to(line, (8, ROWS))
    line = pltpu.roll(line, (mp * HALF - (g % 8) * HALF + ROWS) % ROWS, axis=1)
    lane = lax.broadcasted_iota(I32, (8, ROWS), 1)
    out_ref[ROWS:, :] = jnp.where((lane >= mp * HALF) & (lane < mp * HALF + HALF), line, 0.0)


def backward(
    at_ref,
    mine_ref,
    theirs_ref,
    part_ref,
    other_ref,
    pre_ref,
    hid_ref,
    x_ref,
    w_out_ref,
    loss_ref,
    keep_ref,
    send_ref,
):
    scale = INV_TEMP / (N_FAR * N_QUAD * A_DEV)
    grad_emb = (mine_ref[0:ROWS, :] + theirs_ref[0:ROWS, :]) * scale
    loss_ref[...] = mine_ref[ROWS : ROWS + 1, 0:A_DEV] + theirs_ref[ROWS : ROWS + 1, 0:A_DEV]
    proj = part_ref[...] + other_ref[...]
    norm = norm_of(proj)
    unit = proj / norm
    inner = jnp.sum(unit * grad_emb, axis=1, keepdims=True)
    grad_proj = ((grad_emb - unit * inner) / norm).astype(BF16)
    grad_out = dot(hid_ref[...], grad_proj, ((0,), (0,)))
    grad_hidden = dot(grad_proj, w_out_ref[...], ((1,), (1,)))
    pre = pre_ref[...]
    sig = jax.nn.sigmoid(pre)
    grad_pre = (grad_hidden * sig * (1.0 + pre * (1.0 - sig))).astype(BF16)
    grad_in = dot(x_ref[...], grad_pre, ((0,), (0,)))
    bias = jnp.sum(grad_pre.astype(F32), axis=0, keepdims=True)
    first = lax.broadcasted_iota(I32, (8, 128), 0) == 0
    c = at_ref[1] % 2

    def store(half, out_ref):
        lanes = slice(half * 128, half * 128 + 128)
        for i in range(N_NEAR):
            out_ref[i, 0:32, :] = grad_in[i * 32 : i * 32 + 32, lanes]
            out_ref[i, 32:40, :] = grad_out[half * 128 + i * 8 : half * 128 + i * 8 + 8]
            line = jnp.where(first, bias[:, lanes], 0.0) if i == 0 else jnp.zeros((8, 128), F32)
            out_ref[i, 40:, :] = line

    for side in (0, 1):

        @pl.when(c == side)
        def _():
            store(side, keep_ref)
            store(1 - side, send_ref)


def add(a_ref, b_ref, out_ref):
    out_ref[...] = a_ref[...] + b_ref[...]


def sum_spread(in_ref, out_ref):
    total = jnp.sum(in_ref[...], axis=0)
    for i in range(out_ref.shape[0]):
        out_ref[i] = total


def place(side, in_ref, w_in_ref, w_out_ref, sems):
    lanes = pl.ds(pl.multiple_of(side * 128, 128), 128)
    copies = [
        pltpu.make_async_copy(in_ref.at[:, 0:32, :], w_in_ref.at[:, :, lanes], sems.at[0]),
        pltpu.make_async_copy(in_ref.at[:, 32:40, :], w_out_ref.at[side], sems.at[1]),
    ]
    for copy in copies:
        copy.start()
    return copies


def place_mine(at_ref, mine_ref, loss_in_ref, w_in_ref, w_out_ref, loss_ref, sems):
    copies = place(at_ref[1] % 2, mine_ref, w_in_ref, w_out_ref, sems)
    copies.append(pltpu.make_async_copy(loss_in_ref, loss_ref, sems.at[2]))
    copies[-1].start()
    for copy in copies:
        copy.wait()


def place_theirs(
    at_ref, mine_ref, theirs_ref, _, __, w_in_ref, w_out_ref, b_ref, bias_ref, sems
):
    c = at_ref[1] % 2
    copies = place(1 - c, theirs_ref, w_in_ref, w_out_ref, sems)
    own, other = mine_ref[0, 40:41, :], theirs_ref[0, 40:41, :]
    bias_ref[0:1, :] = jnp.where(c == 0, own, other)
    bias_ref[1:2, :] = jnp.where(c == 0, other, own)
    copies.append(pltpu.make_async_copy(bias_ref, b_ref, sems.at[2]))
    copies[-1].start()
    for copy in copies:
        copy.wait()


def swap(value, axes, flip):
    axes = axes if isinstance(axes, tuple) else (axes,)
    count = lax.axis_size(axes)
    return lax.ppermute(value, axes, [(i, i ^ flip) for i in range(count)])


def exchange(value, axes):
    return lax.all_to_all(value, axes, 0, 0, tiled=True)


def on_device(features, w_in, b_in, w_out, partner, window):
    at = jnp.stack([lax.axis_index(FAR), lax.axis_index(QUAD), lax.axis_index("mp")]).astype(I32)
    part, pre, hidden = call(
        forward,
        [((ROWS, EMB), F32), ((ROWS, 256), F32), ((ROWS, 256), BF16)],
        features,
        w_in,
        b_in.reshape(1, -1),
        w_out,
        first=True,
    )
    other = swap(part, "mp", 1)
    emb, message = call(
        embed,
        [((ROWS, EMB), BF16), ((N_FAR, MSG, EMB), BF16)],
        at,
        window,
        part,
        other,
        partner.reshape(1, -1),
        smem=(0, 1),
        scratch=[pltpu.VMEM((ROWS, EMB), F32)],
    )
    anchors = exchange(message, FAR)
    blocks = [emb] + [swap(emb, QUAD, r) for r in (1, 2, 3)]
    (sums,) = call(totals, [((N_FAR, 8, ROWS), F32)], at, anchors, *blocks, smem=(0,))
    sums = exchange(sums, FAR)
    rows, c0, c1, c2, c3, losses = call(
        weights,
        [((N_FAR, HALF, EMB), F32)] + [((ROWS, EMB), F32)] * 4 + [((8, ROWS), F32)],
        at,
        anchors,
        sums,
        *blocks,
        smem=(0,),
    )
    rows = exchange(rows, FAR)
    r1, r2, r3 = [swap(c, QUAD, r) for r, c in ((1, c1), (2, c2), (3, c3))]
    (mine,) = call(
        gather_rows,
        [((ROWS + 8, EMB), F32)],
        at,
        window,
        rows,
        c0,
        r1,
        r2,
        r3,
        losses,
        smem=(0, 1),
    )
    theirs = swap(mine, "mp", 1)
    half = (N_NEAR, PART, EMB)
    row_loss, keep, send = call(
        backward,
        [((1, A_DEV), F32), (half, F32), (half, F32)],
        at,
        mine,
        theirs,
        part,
        other,
        pre,
        hidden,
        features,
        w_out,
        smem=(0,),
    )
    got = swap(send, "c", 1)
    (both,) = call(add, [(half, F32)], keep, got)
    (both,) = call(sum_spread, [((4, PART, EMB), F32)], exchange(both, NEAR))
    (both,) = call(sum_spread, [(half, F32)], exchange(both, "zh"))
    both = exchange(both, NEAR)
    got = swap(both, "c", 1)
    whole = [((N_NEAR, 32, 256), F32), ((2, N_NEAR, 8, EMB), F32)]
    sems = [pltpu.SemaphoreType.DMA((3,))]
    *grads, row_loss = call(
        place_mine,
        whole + [((1, A_DEV), F32)],
        at,
        both,
        row_loss,
        smem=(0,),
        scratch=sems,
        last=(0, 1, 2),
    )
    grad_in, grad_out, grad_b = call(
        place_theirs,
        whole + [((2, 128), F32)],
        at,
        both,
        got,
        *grads,
        smem=(0,),
        scratch=[pltpu.VMEM((2, 128), F32)] + sems,
        last=(0, 1, 2),
        alias={3: 0, 4: 1},
    )
    return (
        row_loss.reshape(-1),
        grad_in.reshape(512, 256),
        grad_b.reshape(-1),
        grad_out.reshape(256, EMB),
    )


def solution(mesh):
    finer = Mesh(mesh.devices.reshape(*SIZES.values(), mesh.shape["mp"]), (*SIZES, "mp"))
    placed = (P(DP, None), P(None, "mp"), P("mp"), P("mp", None), P(DP), P())
    return jax.shard_map(
        on_device,
        mesh=finer,
        in_specs=placed,
        out_specs=(P(DP), P(None, "mp"), P("mp"), P("mp", None)),
        check_vma=False,
    )
```

```python
import jax
import jax.numpy as jnp
from jax import lax
from jax.experimental import pallas as pl
from jax.experimental.pallas import tpu as pltpu
from jax.sharding import Mesh
from jax.sharding import PartitionSpec as P

SIZES = {"zh": 4, "zl": 2, "x": 4, "yh": 2, "c": 2}
DP = ("zh", "zl", "x", "yh", "c")
NEAR = ("zl", "x", "yh")
FAR = ("zh", "zl", "x")
QUAD = ("yh", "c")

ROWS = 128
A_DEV = 32
HALF = 16
EMB = 128
N_FAR = 32
N_QUAD = 4
ANCHORS = N_FAR * HALF
MSG = 24
PART = 48
N_NEAR = 16

INV_TEMP = 10.0
SHIFT = 10.0
EPS = 1e-06
BF16 = jnp.bfloat16
F32 = jnp.float32
I32 = jnp.int32


def call(kernel, outs, *args, smem=(), scratch=(), first=False, last=(), alias={}):
    specs = [
        pl.BlockSpec(memory_space=pltpu.SMEM if i in smem else pl.ANY if i in alias else pltpu.VMEM)
        for i in range(len(args))
    ]
    if not first:
        args = [
            a if i in smem or i in alias else pltpu.with_memory_space_constraint(a, pltpu.VMEM)
            for i, a in enumerate(args)
        ]
    shapes = [
        jax.ShapeDtypeStruct(s, d) if last else pltpu.VMEM(s, d) for i, (s, d) in enumerate(outs)
    ]
    return pl.pallas_call(
        kernel,
        out_shape=shapes,
        in_specs=specs,
        out_specs=[
            pl.BlockSpec(memory_space=pl.ANY if i in last else pltpu.VMEM) for i in range(len(outs))
        ],
        scratch_shapes=list(scratch),
        input_output_aliases=alias,
    )(*args)


def dot(a, b, dims):
    return lax.dot_general(a, b, (dims, ((), ())), preferred_element_type=F32)


def forward(x_ref, w_in_ref, b_ref, w_out_ref, part_ref, pre_ref, hid_ref):
    pre = dot(x_ref[...], w_in_ref[...], ((1,), (0,))) + b_ref[...]
    hidden = (pre * jax.nn.sigmoid(pre)).astype(BF16)
    pre_ref[...] = pre
    hid_ref[...] = hidden
    part_ref[...] = dot(hidden, w_out_ref[...], ((1,), (0,)))


def norm_of(proj):
    return jnp.sqrt(jnp.sum(proj * proj, axis=1, keepdims=True) + EPS)


def embed(at_ref, window_ref, part_ref, other_ref, partner_ref, emb_ref, msg_ref, hold_ref):
    g, q, mp = at_ref[0], at_ref[1], at_ref[2]
    proj = part_ref[...] + other_ref[...]
    emb = (proj / norm_of(proj)).astype(BF16)
    emb_ref[...] = emb
    hold_ref[...] = emb.astype(F32)
    start = pl.multiple_of(window_ref[g * N_QUAD + q] * A_DEV + mp * HALF, HALF)
    chosen = hold_ref[pl.ds(start, HALF), :]
    to = (g % 8) * HALF
    lane = lax.broadcasted_iota(I32, (8, ROWS), 1)
    row = lax.broadcasted_iota(I32, (8, ROWS), 0)
    partner = jnp.broadcast_to(partner_ref[...], (8, ROWS))
    value = jnp.where(
        row == 0, partner // ROWS, jnp.where(row == 1, partner % ROWS, lane)
    ).astype(F32)
    value = pltpu.roll(value, (to - start + ROWS) % ROWS, axis=1)
    value = jnp.where((lane >= to) & (lane < to + HALF) & (row < 3), value, 0.0)
    message = jnp.concatenate([chosen, value], axis=0).astype(BF16)
    for i in range(N_FAR):
        msg_ref[i] = message


def block_ids(at_ref, msg_ref):
    g, q = at_ref[0], at_ref[1]
    ids = msg_ref[:, HALF:, :].astype(F32)
    ids = ids.reshape(N_FAR // 8, 8, 8, ROWS).sum(axis=1)
    ids = jnp.concatenate([ids[i] for i in range(N_FAR // 8)], axis=1)
    lane = lax.broadcasted_iota(I32, (1, ANCHORS), 1)
    partner = (ids[0:1] * float(ROWS) + ids[1:2]).astype(I32)
    own = (lane // HALF * N_QUAD + q) * ROWS + ids[2:3].astype(I32)
    return partner, own


def column_ids(at_ref, r):
    g, q = at_ref[0], at_ref[1]
    base = (g * N_QUAD + (q ^ r)) * ROWS
    return base + lax.broadcasted_iota(I32, (ROWS, 1), 0)


def anchors_of(msg_ref):
    return jnp.concatenate([msg_ref[i, :HALF, :] for i in range(N_FAR)], axis=0)


def middle_of(anchors):
    return jnp.sum(anchors.astype(F32), axis=0, keepdims=True) * (1.0 / ANCHORS)


def block_sums(at_ref, msg_ref, e0_ref, e1_ref, e2_ref, e3_ref, out_ref):
    anchors = anchors_of(msg_ref)
    partner, own = block_ids(at_ref, msg_ref)
    total = jnp.zeros((1, ANCHORS), F32)
    rows = jnp.zeros((ANCHORS, 2 * EMB), F32)
    pairs = jnp.zeros((ANCHORS, EMB), F32)
    ones = jnp.ones((ROWS, EMB), BF16)
    for r, e_ref in enumerate((e0_ref, e1_ref, e2_ref, e3_ref)):
        cols_emb = e_ref[...]
        s = dot(cols_emb, anchors, ((1,), (1,))) * INV_TEMP
        cols = column_ids(at_ref, r)
        positive = cols == partner
        ex = jnp.where(cols == own, 0.0, jnp.exp(s - SHIFT))
        total = total + jnp.sum(ex, axis=0, keepdims=True)
        others = jnp.where(positive, 0.0, ex).astype(BF16)
        rows = rows + dot(others, jnp.concatenate([cols_emb, ones], axis=1), ((0,), (0,)))
        pairs = pairs + dot(positive.astype(F32).astype(BF16), cols_emb, ((0,), (0,)))
    rows = (rows[:, :EMB] - rows[:, EMB:] * middle_of(anchors)).astype(BF16)
    pairs = pairs.astype(BF16)
    lines = jnp.concatenate([total[:, i * ROWS : (i + 1) * ROWS] for i in range(4)], axis=0)
    high = lines.astype(BF16).astype(F32)
    lines = jnp.concatenate([high, lines - high], axis=0).astype(BF16)
    for i in range(N_FAR):
        here = slice(i * HALF, (i + 1) * HALF)
        out_ref[i, 0:16, :] = rows[here]
        out_ref[i, 16:32, :] = pairs[here]
        out_ref[i, 32:40, :] = lines


def totals_of(sums_ref):
    lines = jnp.sum(sums_ref[:, 32:40, :].astype(F32), axis=0)
    return lines[0:4] + lines[4:8]


def weights(
    at_ref, msg_ref, sums_ref, e0_ref, e1_ref, e2_ref, e3_ref, keep_ref, send_ref
):
    anchors = anchors_of(msg_ref)
    partner, own = block_ids(at_ref, msg_ref)
    total = totals_of(sums_ref)
    total = jnp.concatenate([total[i : i + 1] for i in range(4)], axis=1)
    for r, e_ref in enumerate((e0_ref, e1_ref, e2_ref, e3_ref)):
        s = dot(e_ref[...], anchors, ((1,), (1,))) * INV_TEMP
        cols = column_ids(at_ref, r)
        prob = jnp.where(cols == own, 0.0, jnp.exp(s - SHIFT) / total)
        w = (prob - (cols == partner).astype(F32)).astype(BF16)
        c_ref = send_ref if r % 2 else keep_ref
        c_ref[r // 2] = dot(w, anchors, ((1,), (0,)))


def own_rows(at_ref, msg_ref, sums_ref, out_ref):
    g, mp = at_ref[0], at_ref[2]
    line = lax.broadcasted_iota(I32, (4, ROWS), 0)
    total = jnp.sum(jnp.where(line == g // 8, totals_of(sums_ref), 0.0), axis=0, keepdims=True)
    total = jnp.broadcast_to(total, (HALF, ROWS))
    to = mp * HALF
    total = pltpu.roll(total, (to - (g % 8) * HALF + ROWS) % ROWS, axis=1)
    lane = lax.broadcasted_iota(I32, (HALF, ROWS), 1)
    here = lane == to + lax.broadcasted_iota(I32, (HALF, ROWS), 0)
    pair = jnp.sum(sums_ref[:, 16:32, :].astype(F32), axis=0)
    emb = msg_ref[g, 0:HALF, :].astype(F32)
    hit_of = jnp.sum(emb * pair, axis=1, keepdims=True) * INV_TEMP
    hit = jnp.sum(jnp.where(here, hit_of, 0.0), axis=0, keepdims=True)
    loss = jnp.where((lane >= to) & (lane < to + HALF), jnp.log(total) + SHIFT - hit, 0.0)
    out_ref[HALF:, :] = loss[0:8]
    total_of = jnp.sum(jnp.where(here, total, 0.0), axis=1, keepdims=True)
    ex_pair = jnp.exp(hit_of - SHIFT)
    weight = (ex_pair / total_of - 1.0).astype(BF16).astype(F32)
    rows = jnp.sum(sums_ref[:, 0:16, :].astype(F32), axis=0)
    rows = rows + (total_of - ex_pair) * middle_of(anchors_of(msg_ref))
    out_ref[0:HALF, :] = rows / total_of + weight * pair


def add_pair(a_ref, b_ref, mine_ref, next_ref):
    mine_ref[...] = a_ref[0] + b_ref[0]
    next_ref[...] = a_ref[1] + b_ref[1]


def gather_rows(at_ref, window_ref, rows_ref, c0_ref, c2_ref, out_ref):
    g, q, mp = at_ref[0], at_ref[1], at_ref[2]
    out_ref[0:ROWS, :] = c0_ref[...] + c2_ref[...]
    start = pl.multiple_of(window_ref[g * N_QUAD + q] * A_DEV + mp * HALF, HALF)
    out_ref[pl.ds(start, HALF), :] = out_ref[pl.ds(start, HALF), :] + rows_ref[0:HALF, :]
    out_ref[ROWS:, :] = rows_ref[HALF:, :]


def backward(
    at_ref,
    mine_ref,
    theirs_ref,
    part_ref,
    other_ref,
    pre_ref,
    hid_ref,
    x_ref,
    w_out_ref,
    loss_ref,
    keep_ref,
    send_ref,
):
    scale = INV_TEMP / (N_FAR * N_QUAD * A_DEV)
    grad_emb = (mine_ref[0:ROWS, :] + theirs_ref[0:ROWS, :]) * scale
    loss_ref[...] = mine_ref[ROWS : ROWS + 1, 0:A_DEV] + theirs_ref[ROWS : ROWS + 1, 0:A_DEV]
    proj = part_ref[...] + other_ref[...]
    norm = norm_of(proj)
    unit = proj / norm
    inner = jnp.sum(unit * grad_emb, axis=1, keepdims=True)
    grad_proj = ((grad_emb - unit * inner) / norm).astype(BF16)
    grad_out = dot(hid_ref[...], grad_proj, ((0,), (0,)))
    grad_hidden = dot(grad_proj, w_out_ref[...], ((1,), (1,)))
    pre = pre_ref[...]
    sig = jax.nn.sigmoid(pre)
    grad_pre = (grad_hidden * sig * (1.0 + pre * (1.0 - sig))).astype(BF16)
    grad_in = dot(x_ref[...], grad_pre, ((0,), (0,)))
    bias = jnp.sum(grad_pre.astype(F32), axis=0, keepdims=True)
    first = lax.broadcasted_iota(I32, (8, 128), 0) == 0
    c = at_ref[1] % 2

    def store(half, out_ref):
        lanes = slice(half * 128, half * 128 + 128)
        for i in range(N_NEAR):
            out_ref[i, 0:32, :] = grad_in[i * 32 : i * 32 + 32, lanes]
            out_ref[i, 32:40, :] = grad_out[half * 128 + i * 8 : half * 128 + i * 8 + 8]
            line = jnp.where(first, bias[:, lanes], 0.0) if i == 0 else jnp.zeros((8, 128), F32)
            out_ref[i, 40:, :] = line

    for side in (0, 1):

        @pl.when(c == side)
        def _():
            store(side, keep_ref)
            store(1 - side, send_ref)


def add(a_ref, b_ref, out_ref):
    out_ref[...] = a_ref[...] + b_ref[...]


def sum_spread(in_ref, out_ref):
    total = jnp.sum(in_ref[...], axis=0)
    for i in range(out_ref.shape[0]):
        out_ref[i] = total


def place(side, in_ref, w_in_ref, w_out_ref, sems):
    lanes = pl.ds(pl.multiple_of(side * 128, 128), 128)
    copies = [
        pltpu.make_async_copy(in_ref.at[:, 0:32, :], w_in_ref.at[:, :, lanes], sems.at[0]),
        pltpu.make_async_copy(in_ref.at[:, 32:40, :], w_out_ref.at[side], sems.at[1]),
    ]
    for copy in copies:
        copy.start()
    return copies


def place_mine(at_ref, mine_ref, loss_in_ref, w_in_ref, w_out_ref, loss_ref, sems):
    copies = place(at_ref[1] % 2, mine_ref, w_in_ref, w_out_ref, sems)
    copies.append(pltpu.make_async_copy(loss_in_ref, loss_ref, sems.at[2]))
    copies[-1].start()
    for copy in copies:
        copy.wait()


def place_theirs(
    at_ref, mine_ref, theirs_ref, _, __, w_in_ref, w_out_ref, b_ref, bias_ref, sems
):
    c = at_ref[1] % 2
    copies = place(1 - c, theirs_ref, w_in_ref, w_out_ref, sems)
    own, other = mine_ref[0, 40:41, :], theirs_ref[0, 40:41, :]
    bias_ref[0:1, :] = jnp.where(c == 0, own, other)
    bias_ref[1:2, :] = jnp.where(c == 0, other, own)
    copies.append(pltpu.make_async_copy(bias_ref, b_ref, sems.at[2]))
    copies[-1].start()
    for copy in copies:
        copy.wait()


def swap(value, axes, flip):
    axes = axes if isinstance(axes, tuple) else (axes,)
    count = lax.axis_size(axes)
    return lax.ppermute(value, axes, [(i, i ^ flip) for i in range(count)])


def exchange(value, axes):
    return lax.all_to_all(value, axes, 0, 0, tiled=True)


def on_device(features, w_in, b_in, w_out, partner, window):
    at = jnp.stack([lax.axis_index(FAR), lax.axis_index(QUAD), lax.axis_index("mp")]).astype(I32)
    part, pre, hidden = call(
        forward,
        [((ROWS, EMB), F32), ((ROWS, 256), F32), ((ROWS, 256), BF16)],
        features,
        w_in,
        b_in.reshape(1, -1),
        w_out,
        first=True,
    )
    other = swap(part, "mp", 1)
    emb, message = call(
        embed,
        [((ROWS, EMB), BF16), ((N_FAR, MSG, EMB), BF16)],
        at,
        window,
        part,
        other,
        partner.reshape(1, -1),
        smem=(0, 1),
        scratch=[pltpu.VMEM((ROWS, EMB), F32)],
    )
    anchors = exchange(message, FAR)
    blocks = [emb] + [swap(emb, QUAD, r) for r in (1, 2, 3)]
    (sums,) = call(block_sums, [((N_FAR, 40, EMB), BF16)], at, anchors, *blocks, smem=(0,))
    sums = exchange(sums, FAR)
    pair = (2, ROWS, EMB)
    keep, send = call(
        weights, [(pair, F32), (pair, F32)], at, anchors, sums, *blocks, smem=(0,)
    )
    got = swap(send, "c", 1)
    (rows,) = call(own_rows, [((HALF + 8, EMB), F32)], at, anchors, sums, smem=(0,))
    c0, c2 = call(add_pair, [((ROWS, EMB), F32)] * 2, keep, got)
    c2 = swap(c2, "yh", 1)
    (mine,) = call(
        gather_rows, [((ROWS + 8, EMB), F32)], at, window, rows, c0, c2, smem=(0, 1)
    )
    theirs = swap(mine, "mp", 1)
    half = (N_NEAR, PART, EMB)
    row_loss, keep, send = call(
        backward,
        [((1, A_DEV), F32), (half, F32), (half, F32)],
        at,
        mine,
        theirs,
        part,
        other,
        pre,
        hidden,
        features,
        w_out,
        smem=(0,),
    )
    got = swap(send, "c", 1)
    (both,) = call(add, [(half, F32)], keep, got)
    (both,) = call(sum_spread, [((4, PART, EMB), F32)], exchange(both, NEAR))
    (both,) = call(sum_spread, [(half, F32)], exchange(both, "zh"))
    both = exchange(both, NEAR)
    got = swap(both, "c", 1)
    whole = [((N_NEAR, 32, 256), F32), ((2, N_NEAR, 8, EMB), F32)]
    sems = [pltpu.SemaphoreType.DMA((3,))]
    *grads, row_loss = call(
        place_mine,
        whole + [((1, A_DEV), F32)],
        at,
        both,
        row_loss,
        smem=(0,),
        scratch=sems,
        last=(0, 1, 2),
    )
    grad_in, grad_out, grad_b = call(
        place_theirs,
        whole + [((2, 128), F32)],
        at,
        both,
        got,
        *grads,
        smem=(0,),
        scratch=[pltpu.VMEM((2, 128), F32)] + sems,
        last=(0, 1, 2),
        alias={3: 0, 4: 1},
    )
    return (
        row_loss.reshape(-1),
        grad_in.reshape(512, 256),
        grad_b.reshape(-1),
        grad_out.reshape(256, EMB),
    )


def solution(mesh):
    finer = Mesh(mesh.devices.reshape(*SIZES.values(), mesh.shape["mp"]), (*SIZES, "mp"))
    placed = (P(DP, None), P(None, "mp"), P("mp"), P("mp", None), P(DP), P())
    return jax.shard_map(
        on_device,
        mesh=finer,
        in_specs=placed,
        out_specs=(P(DP), P(None, "mp"), P("mp"), P("mp", None)),
        check_vma=False,
    )
```

```python
import jax
import jax.numpy as jnp
from jax import lax
from jax.experimental import pallas as pl
from jax.experimental.pallas import tpu as pltpu
from jax.sharding import Mesh
from jax.sharding import PartitionSpec as P

SIZES = {"zh": 4, "zl": 2, "x": 4, "yh": 2, "c": 2}
DP = ("zh", "zl", "x", "yh", "c")
NEAR = ("zl", "x", "yh")
FAR = ("zh", "zl", "x")
QUAD = ("yh", "c")

ROWS = 128
A_DEV = 32
HALF = 16
EMB = 128
N_FAR = 32
N_QUAD = 4
ANCHORS = N_FAR * HALF
MSG = 24
PART = 48
N_NEAR = 16

INV_TEMP = 10.0
SHIFT = 10.0
EPS = 1e-06
LOG2E = 1.4426950408889634
BF16 = jnp.bfloat16
F32 = jnp.float32
I32 = jnp.int32


def call(kernel, outs, *args, smem=(), scratch=(), first=False, last=(), alias={}):
    specs = [
        pl.BlockSpec(memory_space=pltpu.SMEM if i in smem else pl.ANY if i in alias else pltpu.VMEM)
        for i in range(len(args))
    ]
    if not first:
        args = [
            a if i in smem or i in alias else pltpu.with_memory_space_constraint(a, pltpu.VMEM)
            for i, a in enumerate(args)
        ]
    shapes = [
        jax.ShapeDtypeStruct(s, d) if last else pltpu.VMEM(s, d) for i, (s, d) in enumerate(outs)
    ]
    return pl.pallas_call(
        kernel,
        out_shape=shapes,
        in_specs=specs,
        out_specs=[
            pl.BlockSpec(memory_space=pl.ANY if i in last else pltpu.VMEM) for i in range(len(outs))
        ],
        scratch_shapes=list(scratch),
        input_output_aliases=alias,
    )(*args)


def dot(a, b, dims):
    return lax.dot_general(a, b, (dims, ((), ())), preferred_element_type=F32)


def forward(x_ref, w_in_ref, b_ref, w_out_ref, part_ref, pre_ref, hid_ref):
    pre = dot(x_ref[...], w_in_ref[...], ((1,), (0,))) + b_ref[...]
    hidden = (pre * jax.nn.sigmoid(pre)).astype(BF16)
    pre_ref[...] = pre
    hid_ref[...] = hidden
    part_ref[...] = dot(hidden, w_out_ref[...], ((1,), (0,)))


def norm_of(proj):
    return jnp.sqrt(jnp.sum(proj * proj, axis=1, keepdims=True) + EPS)


def embed(at_ref, window_ref, part_ref, other_ref, partner_ref, emb_ref, msg_ref, hold_ref):
    g, q, mp = at_ref[0], at_ref[1], at_ref[2]
    proj = part_ref[...] + other_ref[...]
    emb = (proj / norm_of(proj)).astype(BF16)
    emb_ref[...] = emb
    hold_ref[...] = emb.astype(F32)
    start = pl.multiple_of(window_ref[g * N_QUAD + q] * A_DEV + mp * HALF, HALF)
    chosen = hold_ref[pl.ds(start, HALF), :]
    to = (g % 8) * HALF
    lane = lax.broadcasted_iota(I32, (8, ROWS), 1)
    row = lax.broadcasted_iota(I32, (8, ROWS), 0)
    partner = jnp.broadcast_to(partner_ref[...], (8, ROWS))
    value = jnp.where(
        row == 0, partner // ROWS, jnp.where(row == 1, partner % ROWS, lane)
    ).astype(F32)
    value = pltpu.roll(value, (to - start + ROWS) % ROWS, axis=1)
    value = jnp.where((lane >= to) & (lane < to + HALF) & (row < 3), value, 0.0)
    message = jnp.concatenate([chosen, value], axis=0).astype(BF16)
    for i in range(N_FAR):
        msg_ref[i] = message


def block_ids(at_ref, msg_ref):
    g, q = at_ref[0], at_ref[1]
    ids = msg_ref[:, HALF:, :].astype(F32)
    ids = ids.reshape(N_FAR // 8, 8, 8, ROWS).sum(axis=1)
    ids = jnp.concatenate([ids[i] for i in range(N_FAR // 8)], axis=1)
    lane = lax.broadcasted_iota(I32, (1, ANCHORS), 1)
    partner = (ids[0:1] * float(ROWS) + ids[1:2]).astype(I32)
    own = (lane // HALF * N_QUAD + q) * ROWS + ids[2:3].astype(I32)
    return partner, own


def column_ids(at_ref, r):
    g, q = at_ref[0], at_ref[1]
    base = (g * N_QUAD + (q ^ r)) * ROWS
    return base + lax.broadcasted_iota(I32, (ROWS, 1), 0)


def anchors_of(msg_ref):
    return jnp.concatenate([msg_ref[i, :HALF, :] for i in range(N_FAR)], axis=0)


def middle_of(anchors):
    return jnp.sum(anchors.astype(F32), axis=0, keepdims=True) * (1.0 / ANCHORS)


def block_sums(at_ref, msg_ref, e0_ref, e1_ref, e2_ref, e3_ref, out_ref):
    anchors = anchors_of(msg_ref)
    partner, own = block_ids(at_ref, msg_ref)
    total = jnp.zeros((1, ANCHORS), F32)
    rows = jnp.zeros((ANCHORS, 2 * EMB), F32)
    pairs = jnp.zeros((ANCHORS, EMB), F32)
    ones = jnp.ones((ROWS, EMB), BF16)
    for r, e_ref in enumerate((e0_ref, e1_ref, e2_ref, e3_ref)):
        cols_emb = e_ref[...]
        s = dot(cols_emb, anchors, ((1,), (1,)))
        cols = column_ids(at_ref, r)
        positive = cols == partner
        ex = jnp.where(cols == own, 0.0, jnp.exp2(s * (INV_TEMP * LOG2E) - SHIFT * LOG2E))
        total = total + jnp.sum(ex, axis=0, keepdims=True)
        others = jnp.where(positive, 0.0, ex).astype(BF16)
        rows = rows + dot(others, jnp.concatenate([cols_emb, ones], axis=1), ((0,), (0,)))
        pairs = pairs + dot(positive.astype(F32).astype(BF16), cols_emb, ((0,), (0,)))
    rows = (rows[:, :EMB] - rows[:, EMB:] * middle_of(anchors)).astype(BF16)
    pairs = pairs.astype(BF16)
    lines = jnp.concatenate([total[:, i * ROWS : (i + 1) * ROWS] for i in range(4)], axis=0)
    high = lines.astype(BF16).astype(F32)
    lines = jnp.concatenate([high, lines - high], axis=0).astype(BF16)
    for i in range(N_FAR):
        here = slice(i * HALF, (i + 1) * HALF)
        out_ref[i, 0:16, :] = rows[here]
        out_ref[i, 16:32, :] = pairs[here]
        out_ref[i, 32:40, :] = lines


def totals_of(sums_ref):
    lines = jnp.sum(sums_ref[:, 32:40, :].astype(F32), axis=0)
    return lines[0:4] + lines[4:8]


def weights(
    at_ref, msg_ref, sums_ref, e0_ref, e1_ref, e2_ref, e3_ref, keep_ref, send_ref
):
    anchors = anchors_of(msg_ref)
    partner, own = block_ids(at_ref, msg_ref)
    total = totals_of(sums_ref)
    total = jnp.concatenate([total[i : i + 1] for i in range(4)], axis=1)
    offset = SHIFT * LOG2E + jnp.log2(total)
    for r, e_ref in enumerate((e0_ref, e1_ref, e2_ref, e3_ref)):
        s = dot(e_ref[...], anchors, ((1,), (1,)))
        cols = column_ids(at_ref, r)
        prob = jnp.where(cols == own, 0.0, jnp.exp2(s * (INV_TEMP * LOG2E) - offset))
        w = jnp.where(cols == partner, prob - 1.0, prob).astype(BF16)
        c_ref = send_ref if r % 2 else keep_ref
        c_ref[r // 2] = dot(w, anchors, ((1,), (0,)))


def own_rows(at_ref, msg_ref, sums_ref, out_ref):
    g, mp = at_ref[0], at_ref[2]
    line = lax.broadcasted_iota(I32, (4, ROWS), 0)
    total = jnp.sum(jnp.where(line == g // 8, totals_of(sums_ref), 0.0), axis=0, keepdims=True)
    total = jnp.broadcast_to(total, (HALF, ROWS))
    to = mp * HALF
    total = pltpu.roll(total, (to - (g % 8) * HALF + ROWS) % ROWS, axis=1)
    lane = lax.broadcasted_iota(I32, (HALF, ROWS), 1)
    here = lane == to + lax.broadcasted_iota(I32, (HALF, ROWS), 0)
    pair = jnp.sum(sums_ref[:, 16:32, :].astype(F32), axis=0)
    emb = msg_ref[g, 0:HALF, :].astype(F32)
    hit_of = jnp.sum(emb * pair, axis=1, keepdims=True) * INV_TEMP
    hit = jnp.sum(jnp.where(here, hit_of, 0.0), axis=0, keepdims=True)
    loss = jnp.where((lane >= to) & (lane < to + HALF), jnp.log(total) + SHIFT - hit, 0.0)
    out_ref[HALF:, :] = loss[0:8]
    total_of = jnp.sum(jnp.where(here, total, 0.0), axis=1, keepdims=True)
    ex_pair = jnp.exp(hit_of - SHIFT)
    weight = (ex_pair / total_of - 1.0).astype(BF16).astype(F32)
    rows = jnp.sum(sums_ref[:, 0:16, :].astype(F32), axis=0)
    rows = rows + (total_of - ex_pair) * middle_of(anchors_of(msg_ref))
    out_ref[0:HALF, :] = rows / total_of + weight * pair


def add_pair(at_ref, window_ref, a_ref, b_ref, rows_ref, mine_ref, next_ref):
    g, q, mp = at_ref[0], at_ref[1], at_ref[2]
    mine_ref[0:ROWS, :] = a_ref[0] + b_ref[0]
    next_ref[...] = a_ref[1] + b_ref[1]
    start = pl.multiple_of(window_ref[g * N_QUAD + q] * A_DEV + mp * HALF, HALF)
    mine_ref[pl.ds(start, HALF), :] = mine_ref[pl.ds(start, HALF), :] + rows_ref[0:HALF, :]
    mine_ref[ROWS:, :] = rows_ref[HALF:, :]


def backward(
    at_ref,
    mine_ref,
    theirs_ref,
    third_ref,
    fourth_ref,
    part_ref,
    other_ref,
    pre_ref,
    hid_ref,
    x_ref,
    w_out_ref,
    loss_ref,
    keep_ref,
    send_ref,
):
    scale = INV_TEMP / (N_FAR * N_QUAD * A_DEV)
    grad_emb = mine_ref[0:ROWS, :] + theirs_ref[0:ROWS, :]
    grad_emb = (grad_emb + (third_ref[...] + fourth_ref[...])) * scale
    loss_ref[...] = mine_ref[ROWS : ROWS + 1, 0:A_DEV] + theirs_ref[ROWS : ROWS + 1, 0:A_DEV]
    proj = part_ref[...] + other_ref[...]
    norm = norm_of(proj)
    unit = proj / norm
    inner = jnp.sum(unit * grad_emb, axis=1, keepdims=True)
    grad_proj = ((grad_emb - unit * inner) / norm).astype(BF16)
    grad_out = dot(hid_ref[...], grad_proj, ((0,), (0,)))
    grad_hidden = dot(grad_proj, w_out_ref[...], ((1,), (1,)))
    pre = pre_ref[...]
    sig = jax.nn.sigmoid(pre)
    grad_pre = (grad_hidden * sig * (1.0 + pre * (1.0 - sig))).astype(BF16)
    grad_in = dot(x_ref[...], grad_pre, ((0,), (0,)))
    bias = jnp.sum(grad_pre.astype(F32), axis=0, keepdims=True)
    first = lax.broadcasted_iota(I32, (8, 128), 0) == 0
    c = at_ref[1] % 2

    def store(half, out_ref):
        lanes = slice(half * 128, half * 128 + 128)
        for i in range(N_NEAR):
            out_ref[i, 0:32, :] = grad_in[i * 32 : i * 32 + 32, lanes]
            out_ref[i, 32:40, :] = grad_out[half * 128 + i * 8 : half * 128 + i * 8 + 8]
            line = jnp.where(first, bias[:, lanes], 0.0) if i == 0 else jnp.zeros((8, 128), F32)
            out_ref[i, 40:, :] = line

    for side in (0, 1):

        @pl.when(c == side)
        def _():
            store(side, keep_ref)
            store(1 - side, send_ref)


def add(a_ref, b_ref, out_ref):
    out_ref[...] = a_ref[...] + b_ref[...]


def sum_spread(in_ref, out_ref):
    total = jnp.sum(in_ref[...], axis=0)
    for i in range(out_ref.shape[0]):
        out_ref[i] = total


def place(side, in_ref, w_in_ref, w_out_ref, sems):
    lanes = pl.ds(pl.multiple_of(side * 128, 128), 128)
    copies = [
        pltpu.make_async_copy(in_ref.at[:, 0:32, :], w_in_ref.at[:, :, lanes], sems.at[0]),
        pltpu.make_async_copy(in_ref.at[:, 32:40, :], w_out_ref.at[side], sems.at[1]),
    ]
    for copy in copies:
        copy.start()
    return copies


def place_mine(at_ref, mine_ref, loss_in_ref, w_in_ref, w_out_ref, loss_ref, sems):
    copies = place(at_ref[1] % 2, mine_ref, w_in_ref, w_out_ref, sems)
    copies.append(pltpu.make_async_copy(loss_in_ref, loss_ref, sems.at[2]))
    copies[-1].start()
    for copy in copies:
        copy.wait()


def place_theirs(
    at_ref, mine_ref, theirs_ref, _, __, w_in_ref, w_out_ref, b_ref, bias_ref, sems
):
    c = at_ref[1] % 2
    copies = place(1 - c, theirs_ref, w_in_ref, w_out_ref, sems)
    own, other = mine_ref[0, 40:41, :], theirs_ref[0, 40:41, :]
    bias_ref[0:1, :] = jnp.where(c == 0, own, other)
    bias_ref[1:2, :] = jnp.where(c == 0, other, own)
    copies.append(pltpu.make_async_copy(bias_ref, b_ref, sems.at[2]))
    copies[-1].start()
    for copy in copies:
        copy.wait()


def swap(value, axes, flip):
    axes = axes if isinstance(axes, tuple) else (axes,)
    count = lax.axis_size(axes)
    return lax.ppermute(value, axes, [(i, i ^ flip) for i in range(count)])


def exchange(value, axes):
    return lax.all_to_all(value, axes, 0, 0, tiled=True)


def on_device(features, w_in, b_in, w_out, partner, window):
    at = jnp.stack([lax.axis_index(FAR), lax.axis_index(QUAD), lax.axis_index("mp")]).astype(I32)
    part, pre, hidden = call(
        forward,
        [((ROWS, EMB), F32), ((ROWS, 256), F32), ((ROWS, 256), BF16)],
        features,
        w_in,
        b_in.reshape(1, -1),
        w_out,
        first=True,
    )
    other = swap(part, "mp", 1)
    emb, message = call(
        embed,
        [((ROWS, EMB), BF16), ((N_FAR, MSG, EMB), BF16)],
        at,
        window,
        part,
        other,
        partner.reshape(1, -1),
        smem=(0, 1),
        scratch=[pltpu.VMEM((ROWS, EMB), F32)],
    )
    anchors = exchange(message, FAR)
    blocks = [emb] + [swap(emb, QUAD, r) for r in (1, 2, 3)]
    (sums,) = call(block_sums, [((N_FAR, 40, EMB), BF16)], at, anchors, *blocks, smem=(0,))
    sums = exchange(sums, FAR)
    pair = (2, ROWS, EMB)
    keep, send = call(
        weights, [(pair, F32), (pair, F32)], at, anchors, sums, *blocks, smem=(0,)
    )
    got = swap(send, "c", 1)
    (rows,) = call(own_rows, [((HALF + 8, EMB), F32)], at, anchors, sums, smem=(0,))
    mine, away = call(
        add_pair,
        [((ROWS + 8, EMB), F32), ((ROWS, EMB), F32)],
        at,
        window,
        keep,
        got,
        rows,
        smem=(0, 1),
    )
    third = swap(away, "yh", 1)
    fourth = swap(away, ("yh", "mp"), 3)
    theirs = swap(mine, "mp", 1)
    half = (N_NEAR, PART, EMB)
    row_loss, keep, send = call(
        backward,
        [((1, A_DEV), F32), (half, F32), (half, F32)],
        at,
        mine,
        theirs,
        third,
        fourth,
        part,
        other,
        pre,
        hidden,
        features,
        w_out,
        smem=(0,),
    )
    got = swap(send, "c", 1)
    (both,) = call(add, [(half, F32)], keep, got)
    (both,) = call(sum_spread, [((4, PART, EMB), F32)], exchange(both, NEAR))
    (both,) = call(sum_spread, [(half, F32)], exchange(both, "zh"))
    both = exchange(both, NEAR)
    got = swap(both, "c", 1)
    whole = [((N_NEAR, 32, 256), F32), ((2, N_NEAR, 8, EMB), F32)]
    sems = [pltpu.SemaphoreType.DMA((3,))]
    *grads, row_loss = call(
        place_mine,
        whole + [((1, A_DEV), F32)],
        at,
        both,
        row_loss,
        smem=(0,),
        scratch=sems,
        last=(0, 1, 2),
    )
    grad_in, grad_out, grad_b = call(
        place_theirs,
        whole + [((2, 128), F32)],
        at,
        both,
        got,
        *grads,
        smem=(0,),
        scratch=[pltpu.VMEM((2, 128), F32)] + sems,
        last=(0, 1, 2),
        alias={3: 0, 4: 1},
    )
    return (
        row_loss.reshape(-1),
        grad_in.reshape(512, 256),
        grad_b.reshape(-1),
        grad_out.reshape(256, EMB),
    )


def solution(mesh):
    finer = Mesh(mesh.devices.reshape(*SIZES.values(), mesh.shape["mp"]), (*SIZES, "mp"))
    placed = (P(DP, None), P(None, "mp"), P("mp"), P("mp", None), P(DP), P())
    return jax.shard_map(
        on_device,
        mesh=finer,
        in_specs=placed,
        out_specs=(P(DP), P(None, "mp"), P("mp"), P("mp", None)),
        check_vma=False,
    )
```

```python
import jax
import jax.numpy as jnp
from jax import lax
from jax.experimental import pallas as pl
from jax.experimental.pallas import tpu as pltpu
from jax.sharding import Mesh
from jax.sharding import PartitionSpec as P

SIZES = {"zh": 4, "zl": 2, "x": 4, "yh": 2, "c": 2}
DP = ("zh", "zl", "x", "yh", "c")
NEAR = ("zl", "x", "yh")
FAR = ("zh", "zl", "x")
QUAD = ("yh", "c")

ROWS = 128
A_DEV = 32
HALF = 16
EMB = 128
N_FAR = 32
N_QUAD = 4
ANCHORS = N_FAR * HALF
MSG = 24
PART = 48
N_NEAR = 16

INV_TEMP = 10.0
SHIFT = 10.0
EPS = 1e-06
LOG2E = 1.4426950408889634
BF16 = jnp.bfloat16
F32 = jnp.float32
I32 = jnp.int32


def call(kernel, outs, *args, scratch=(), first=False, last=(), alias={}):
    specs = [
        pl.BlockSpec(memory_space=pl.ANY if i in alias else pltpu.VMEM) for i in range(len(args))
    ]
    if not first:
        args = [
            a if i in alias else pltpu.with_memory_space_constraint(a, pltpu.VMEM)
            for i, a in enumerate(args)
        ]
    shapes = [
        jax.ShapeDtypeStruct(s, d) if last else pltpu.VMEM(s, d) for i, (s, d) in enumerate(outs)
    ]
    return pl.pallas_call(
        kernel,
        out_shape=shapes,
        in_specs=specs,
        out_specs=[
            pl.BlockSpec(memory_space=pl.ANY if i in last else pltpu.VMEM) for i in range(len(outs))
        ],
        scratch_shapes=list(scratch),
        input_output_aliases=alias,
    )(*args)


def place_of():
    return lax.axis_index(FAR), lax.axis_index(QUAD), lax.axis_index("mp")


def start_of(window_ref):
    g, q, mp = place_of()
    lane = lax.broadcasted_iota(I32, (1, ROWS), 1)
    block = jnp.where(lane == g * N_QUAD + q, window_ref[...], 0)
    return jnp.sum(block, axis=1, keepdims=True) * A_DEV + mp * HALF


def dot(a, b, dims):
    return lax.dot_general(a, b, (dims, ((), ())), preferred_element_type=F32)


def forward(
    x_ref, w_in_ref, b_ref, w_out_ref, *refs
):
    partner_ref, window_ref, part_ref, pre_ref, hid_ref, partner_out_ref, window_out_ref = refs
    partner_out_ref[...] = partner_ref[...]
    window_out_ref[...] = window_ref[...]
    pre = dot(x_ref[...], w_in_ref[...], ((1,), (0,))) + b_ref[...]
    hidden = (pre * jax.nn.sigmoid(pre)).astype(BF16)
    pre_ref[...] = pre
    hid_ref[...] = hidden
    part_ref[...] = dot(hidden, w_out_ref[...], ((1,), (0,)))


def norm_of(proj):
    return jnp.sqrt(jnp.sum(proj * proj, axis=1, keepdims=True) + EPS)


def embed(window_ref, part_ref, other_ref, partner_ref, emb_ref, msg_ref):
    g, q, mp = place_of()
    proj = part_ref[...] + other_ref[...]
    rounded = (proj / norm_of(proj)).astype(BF16)
    emb_ref[...] = rounded
    emb = rounded.astype(F32)
    start = start_of(window_ref)
    to = (g % 8) * HALF
    lane = lax.broadcasted_iota(I32, (8, ROWS), 1)
    row = lax.broadcasted_iota(I32, (8, ROWS), 0)
    partner = jnp.broadcast_to(partner_ref[...], (8, ROWS))
    ids = jnp.where(
        row == 0, partner // ROWS, jnp.where(row == 1, partner % ROWS, lane)
    ).astype(F32)
    chosen = jnp.zeros((HALF, EMB), F32)
    value = jnp.zeros((8, ROWS), F32)
    for at in range(0, ROWS, HALF):
        chosen = chosen + jnp.where(start == at, emb[at : at + HALF], 0.0)
        value = value + jnp.where(start == at, pltpu.roll(ids, (ROWS - at) % ROWS, axis=1), 0.0)
    value = jnp.where((lane < HALF) & (row < 3), value, 0.0)
    value = pltpu.roll(value, to, axis=1)
    message = jnp.concatenate([chosen, value], axis=0).astype(BF16)
    for i in range(N_FAR):
        msg_ref[i] = message


def block_ids(msg_ref):
    _, q, _ = place_of()
    ids = msg_ref[:, HALF:, :].astype(F32)
    ids = ids.reshape(N_FAR // 8, 8, 8, ROWS).sum(axis=1)
    ids = jnp.concatenate([ids[i] for i in range(N_FAR // 8)], axis=1)
    lane = lax.broadcasted_iota(I32, (1, ANCHORS), 1)
    partner = (ids[0:1] * float(ROWS) + ids[1:2]).astype(I32)
    own = (lane // HALF * N_QUAD + q) * ROWS + ids[2:3].astype(I32)
    return partner, own


def column_ids(r):
    g, q, _ = place_of()
    base = (g * N_QUAD + (q ^ r)) * ROWS
    return base + lax.broadcasted_iota(I32, (ROWS, 1), 0)


def anchors_of(msg_ref):
    return jnp.concatenate([msg_ref[i, :HALF, :] for i in range(N_FAR)], axis=0)


def middle_of(anchors):
    return jnp.sum(anchors.astype(F32), axis=0, keepdims=True) * (1.0 / ANCHORS)


def block_sums(msg_ref, e0_ref, e1_ref, e2_ref, e3_ref, out_ref):
    anchors = anchors_of(msg_ref)
    partner, own = block_ids(msg_ref)
    total = jnp.zeros((1, ANCHORS), F32)
    rows = jnp.zeros((ANCHORS, 2 * EMB), F32)
    pairs = jnp.zeros((ANCHORS, EMB), F32)
    ones = jnp.ones((ROWS, EMB), BF16)
    for r, e_ref in enumerate((e0_ref, e1_ref, e2_ref, e3_ref)):
        cols_emb = e_ref[...]
        s = dot(cols_emb, anchors, ((1,), (1,)))
        cols = column_ids(r)
        positive = cols == partner
        ex = jnp.where(cols == own, 0.0, jnp.exp2(s * (INV_TEMP * LOG2E) - SHIFT * LOG2E))
        total = total + jnp.sum(ex, axis=0, keepdims=True)
        others = jnp.where(positive, 0.0, ex).astype(BF16)
        rows = rows + dot(others, jnp.concatenate([cols_emb, ones], axis=1), ((0,), (0,)))
        pairs = pairs + dot(positive.astype(F32).astype(BF16), cols_emb, ((0,), (0,)))
    rows = (rows[:, :EMB] - rows[:, EMB:] * middle_of(anchors)).astype(BF16)
    pairs = pairs.astype(BF16)
    lines = jnp.concatenate([total[:, i * ROWS : (i + 1) * ROWS] for i in range(4)], axis=0)
    high = lines.astype(BF16).astype(F32)
    lines = jnp.concatenate([high, lines - high], axis=0).astype(BF16)
    for i in range(N_FAR):
        here = slice(i * HALF, (i + 1) * HALF)
        out_ref[i, 0:16, :] = rows[here]
        out_ref[i, 16:32, :] = pairs[here]
        out_ref[i, 32:40, :] = lines


def totals_of(sums_ref):
    lines = jnp.sum(sums_ref[:, 32:40, :].astype(F32), axis=0)
    return lines[0:4] + lines[4:8]


def weights(
    msg_ref, sums_ref, e0_ref, e1_ref, e2_ref, e3_ref, keep_ref, send_ref
):
    anchors = anchors_of(msg_ref)
    partner, own = block_ids(msg_ref)
    total = totals_of(sums_ref)
    total = jnp.concatenate([total[i : i + 1] for i in range(4)], axis=1)
    offset = SHIFT * LOG2E + jnp.log2(total)
    for r, e_ref in enumerate((e0_ref, e1_ref, e2_ref, e3_ref)):
        s = dot(e_ref[...], anchors, ((1,), (1,)))
        cols = column_ids(r)
        prob = jnp.where(cols == own, 0.0, jnp.exp2(s * (INV_TEMP * LOG2E) - offset))
        w = jnp.where(cols == partner, prob - 1.0, prob).astype(BF16)
        c_ref = send_ref if r % 2 else keep_ref
        c_ref[r // 2] = dot(w, anchors, ((1,), (0,)))


def own_rows(msg_ref, sums_ref, out_ref):
    g, _, mp = place_of()
    line = lax.broadcasted_iota(I32, (4, ROWS), 0)
    total = jnp.sum(jnp.where(line == g // 8, totals_of(sums_ref), 0.0), axis=0, keepdims=True)
    total = jnp.broadcast_to(total, (HALF, ROWS))
    to = mp * HALF
    total = pltpu.roll(total, (to - (g % 8) * HALF + ROWS) % ROWS, axis=1)
    lane = lax.broadcasted_iota(I32, (HALF, ROWS), 1)
    here = lane == to + lax.broadcasted_iota(I32, (HALF, ROWS), 0)
    pair = jnp.sum(sums_ref[:, 16:32, :].astype(F32), axis=0)
    emb = msg_ref[g, 0:HALF, :].astype(F32)
    hit_of = jnp.sum(emb * pair, axis=1, keepdims=True) * INV_TEMP
    hit = jnp.sum(jnp.where(here, hit_of, 0.0), axis=0, keepdims=True)
    loss = jnp.where((lane >= to) & (lane < to + HALF), jnp.log(total) + SHIFT - hit, 0.0)
    out_ref[HALF:, :] = loss[0:8]
    total_of = jnp.sum(jnp.where(here, total, 0.0), axis=1, keepdims=True)
    ex_pair = jnp.exp(hit_of - SHIFT)
    weight = (ex_pair / total_of - 1.0).astype(BF16).astype(F32)
    rows = jnp.sum(sums_ref[:, 0:16, :].astype(F32), axis=0)
    rows = rows + (total_of - ex_pair) * middle_of(anchors_of(msg_ref))
    out_ref[0:HALF, :] = rows / total_of + weight * pair


def add_pair(window_ref, a_ref, b_ref, rows_ref, mine_ref, next_ref):
    next_ref[...] = a_ref[1] + b_ref[1]
    start = start_of(window_ref)
    rows = rows_ref[0:HALF, :]
    for at in range(0, ROWS, HALF):
        here = slice(at, at + HALF)
        mine_ref[here, :] = a_ref[0, here] + b_ref[0, here] + jnp.where(start == at, rows, 0.0)
    mine_ref[ROWS:, :] = rows_ref[HALF:, :]


def backward(
    mine_ref,
    theirs_ref,
    third_ref,
    fourth_ref,
    part_ref,
    other_ref,
    pre_ref,
    hid_ref,
    x_ref,
    w_out_ref,
    loss_ref,
    keep_ref,
    send_ref,
):
    scale = INV_TEMP / (N_FAR * N_QUAD * A_DEV)
    grad_emb = mine_ref[0:ROWS, :] + theirs_ref[0:ROWS, :]
    grad_emb = (grad_emb + (third_ref[...] + fourth_ref[...])) * scale
    loss_ref[...] = mine_ref[ROWS : ROWS + 1, 0:A_DEV] + theirs_ref[ROWS : ROWS + 1, 0:A_DEV]
    proj = part_ref[...] + other_ref[...]
    norm = norm_of(proj)
    unit = proj / norm
    inner = jnp.sum(unit * grad_emb, axis=1, keepdims=True)
    grad_proj = ((grad_emb - unit * inner) / norm).astype(BF16)
    grad_out = dot(hid_ref[...], grad_proj, ((0,), (0,)))
    grad_hidden = dot(grad_proj, w_out_ref[...], ((1,), (1,)))
    pre = pre_ref[...]
    sig = jax.nn.sigmoid(pre)
    grad_pre = (grad_hidden * sig * (1.0 + pre * (1.0 - sig))).astype(BF16)
    grad_in = dot(x_ref[...], grad_pre, ((0,), (0,)))
    bias = jnp.sum(grad_pre.astype(F32), axis=0, keepdims=True)
    first = lax.broadcasted_iota(I32, (8, 128), 0) == 0
    c = lax.axis_index("c")

    def store(half, out_ref):
        lanes = slice(half * 128, half * 128 + 128)
        for i in range(N_NEAR):
            out_ref[i, 0:32, :] = grad_in[i * 32 : i * 32 + 32, lanes]
            out_ref[i, 32:40, :] = grad_out[half * 128 + i * 8 : half * 128 + i * 8 + 8]
            line = jnp.where(first, bias[:, lanes], 0.0) if i == 0 else jnp.zeros((8, 128), F32)
            out_ref[i, 40:, :] = line

    for side in (0, 1):

        @pl.when(c == side)
        def _():
            store(side, keep_ref)
            store(1 - side, send_ref)


def add(a_ref, b_ref, out_ref):
    out_ref[...] = a_ref[...] + b_ref[...]


def sum_spread(in_ref, out_ref):
    total = jnp.sum(in_ref[...], axis=0)
    for i in range(out_ref.shape[0]):
        out_ref[i] = total


def place(side, in_ref, w_in_ref, w_out_ref, sems):
    lanes = pl.ds(pl.multiple_of(side * 128, 128), 128)
    copies = [
        pltpu.make_async_copy(in_ref.at[:, 0:32, :], w_in_ref.at[:, :, lanes], sems.at[0]),
        pltpu.make_async_copy(in_ref.at[:, 32:40, :], w_out_ref.at[side], sems.at[1]),
    ]
    for copy in copies:
        copy.start()
    return copies


def place_mine(mine_ref, loss_in_ref, w_in_ref, w_out_ref, loss_ref, sems):
    copies = place(lax.axis_index("c"), mine_ref, w_in_ref, w_out_ref, sems)
    copies.append(pltpu.make_async_copy(loss_in_ref, loss_ref, sems.at[2]))
    copies[-1].start()
    for copy in copies:
        copy.wait()


def place_theirs(
    mine_ref, theirs_ref, _, __, w_in_ref, w_out_ref, b_ref, bias_ref, sems
):
    c = lax.axis_index("c")
    copies = place(1 - c, theirs_ref, w_in_ref, w_out_ref, sems)
    own, other = mine_ref[0, 40:41, :], theirs_ref[0, 40:41, :]
    bias_ref[0:1, :] = jnp.where(c == 0, own, other)
    bias_ref[1:2, :] = jnp.where(c == 0, other, own)
    copies.append(pltpu.make_async_copy(bias_ref, b_ref, sems.at[2]))
    copies[-1].start()
    for copy in copies:
        copy.wait()


def swap(value, axes, flip):
    axes = axes if isinstance(axes, tuple) else (axes,)
    count = lax.axis_size(axes)
    return lax.ppermute(value, axes, [(i, i ^ flip) for i in range(count)])


def exchange(value, axes):
    return lax.all_to_all(value, axes, 0, 0, tiled=True)


def on_device(features, w_in, b_in, w_out, partner, window):
    line = (1, ROWS)
    part, pre, hidden, partner, window = call(
        forward,
        [((ROWS, EMB), F32), ((ROWS, 256), F32), ((ROWS, 256), BF16), (line, I32), (line, I32)],
        features,
        w_in,
        b_in.reshape(1, -1),
        w_out,
        partner.reshape(line),
        window.reshape(line),
        first=True,
    )
    other = swap(part, "mp", 1)
    emb, message = call(
        embed,
        [((ROWS, EMB), BF16), ((N_FAR, MSG, EMB), BF16)],
        window,
        part,
        other,
        partner,
    )
    anchors = exchange(message, FAR)
    blocks = [emb] + [swap(emb, QUAD, r) for r in (1, 2, 3)]
    (sums,) = call(block_sums, [((N_FAR, 40, EMB), BF16)], anchors, *blocks)
    sums = exchange(sums, FAR)
    pair = (2, ROWS, EMB)
    keep, send = call(weights, [(pair, F32), (pair, F32)], anchors, sums, *blocks)
    got = swap(send, "c", 1)
    (rows,) = call(own_rows, [((HALF + 8, EMB), F32)], anchors, sums)
    mine, away = call(
        add_pair,
        [((ROWS + 8, EMB), F32), ((ROWS, EMB), F32)],
        window,
        keep,
        got,
        rows,
    )
    third = swap(away, "yh", 1)
    fourth = swap(away, ("yh", "mp"), 3)
    theirs = swap(mine, "mp", 1)
    half = (N_NEAR, PART, EMB)
    row_loss, keep, send = call(
        backward,
        [((1, A_DEV), F32), (half, F32), (half, F32)],
        mine,
        theirs,
        third,
        fourth,
        part,
        other,
        pre,
        hidden,
        features,
        w_out,
    )
    got = swap(send, "c", 1)
    (both,) = call(add, [(half, F32)], keep, got)
    (both,) = call(sum_spread, [((4, PART, EMB), F32)], exchange(both, NEAR))
    (both,) = call(sum_spread, [(half, F32)], exchange(both, "zh"))
    both = exchange(both, NEAR)
    got = swap(both, "c", 1)
    whole = [((N_NEAR, 32, 256), F32), ((2, N_NEAR, 8, EMB), F32)]
    sems = [pltpu.SemaphoreType.DMA((3,))]
    *grads, row_loss = call(
        place_mine,
        whole + [((1, A_DEV), F32)],
        both,
        row_loss,
        scratch=sems,
        last=(0, 1, 2),
    )
    grad_in, grad_out, grad_b = call(
        place_theirs,
        whole + [((2, 128), F32)],
        both,
        got,
        *grads,
        scratch=[pltpu.VMEM((2, 128), F32)] + sems,
        last=(0, 1, 2),
        alias={2: 0, 3: 1},
    )
    return (
        row_loss.reshape(-1),
        grad_in.reshape(512, 256),
        grad_b.reshape(-1),
        grad_out.reshape(256, EMB),
    )


def solution(mesh):
    finer = Mesh(mesh.devices.reshape(*SIZES.values(), mesh.shape["mp"]), (*SIZES, "mp"))
    placed = (P(DP, None), P(None, "mp"), P("mp"), P("mp", None), P(DP), P())
    return jax.shard_map(
        on_device,
        mesh=finer,
        in_specs=placed,
        out_specs=(P(DP), P(None, "mp"), P("mp"), P("mp", None)),
        check_vma=False,
    )
```

```python
import jax
import jax.numpy as jnp
from jax import lax
from jax.experimental import pallas as pl
from jax.experimental.pallas import tpu as pltpu
from jax.sharding import Mesh
from jax.sharding import PartitionSpec as P


SIZES = {"zh": 4, "zl": 2, "x": 4, "yh": 2, "c": 2}
DP = ("zh", "zl", "x", "yh", "c")
NEAR = ("yh", "x", "zl")
FAR = ("zh", "zl", "x")
QUAD = ("yh", "c")

ROWS = 128
A_DEV = 32
HALF = 16
EMB = 128
N_FAR = 32
N_QUAD = 4
ANCHORS = N_FAR * HALF
MSG = 24
PART = 48
N_NEAR = 16

INV_TEMP = 10.0
SHIFT = 10.0
EPS = 1e-06
LOG2E = 1.4426950408889634
BF16 = jnp.bfloat16
F32 = jnp.float32
I32 = jnp.int32


def call(kernel, outs, *args, scratch=(), first=False, last=(), alias={}):
    specs = [
        pl.BlockSpec(memory_space=pl.ANY if i in alias else pltpu.VMEM) for i in range(len(args))
    ]
    if not first:
        args = [
            a if i in alias else pltpu.with_memory_space_constraint(a, pltpu.VMEM)
            for i, a in enumerate(args)
        ]
    shapes = [jax.ShapeDtypeStruct(s, d) if last else pltpu.VMEM(s, d) for s, d in outs]
    return pl.pallas_call(
        kernel,
        out_shape=shapes,
        in_specs=specs,
        out_specs=[
            pl.BlockSpec(memory_space=pl.ANY if i in last else pltpu.VMEM) for i in range(len(outs))
        ],
        scratch_shapes=list(scratch),
        input_output_aliases=alias,
    )(*args)


def place_of():
    return lax.axis_index(FAR), lax.axis_index(QUAD), lax.axis_index("mp")


def start_of(window_ref):
    g, q, mp = place_of()
    lane = lax.broadcasted_iota(I32, (1, ROWS), 1)
    block = jnp.where(lane == g * N_QUAD + q, window_ref[...], 0)
    return jnp.sum(block, axis=1, keepdims=True) * A_DEV + mp * HALF


def dot(a, b, dims):
    return lax.dot_general(a, b, (dims, ((), ())), preferred_element_type=F32)


def forward(
    x_ref, w_in_ref, b_ref, w_out_ref, *refs
):
    partner_ref, window_ref, part_ref, pre_ref, hid_ref, partner_out_ref, window_out_ref = refs
    partner_out_ref[...] = partner_ref[...]
    window_out_ref[...] = window_ref[...]
    pre = dot(x_ref[...], w_in_ref[...], ((1,), (0,))) + b_ref[...]
    hidden = (pre * jax.nn.sigmoid(pre)).astype(BF16)
    pre_ref[...] = pre
    hid_ref[...] = hidden
    part_ref[...] = dot(hidden, w_out_ref[...], ((1,), (0,)))


def norm_of(proj):
    return jnp.sqrt(jnp.sum(proj * proj, axis=1, keepdims=True) + EPS)


def embed(window_ref, part_ref, other_ref, partner_ref, emb_ref, msg_ref):
    g, _, _ = place_of()
    proj = part_ref[...] + other_ref[...]
    rounded = (proj / norm_of(proj)).astype(BF16)
    emb_ref[...] = rounded
    emb = rounded.astype(F32)
    start = start_of(window_ref)
    to = (g % 8) * HALF
    lane = lax.broadcasted_iota(I32, (8, ROWS), 1)
    row = lax.broadcasted_iota(I32, (8, ROWS), 0)
    partner = jnp.broadcast_to(partner_ref[...], (8, ROWS))
    ids = jnp.where(
        row == 0, partner // ROWS, jnp.where(row == 1, partner % ROWS, lane)
    ).astype(F32)
    chosen = jnp.zeros((HALF, EMB), F32)
    value = jnp.zeros((8, ROWS), F32)
    for at in range(0, ROWS, HALF):
        chosen = chosen + jnp.where(start == at, emb[at : at + HALF], 0.0)
        value = value + jnp.where(start == at, pltpu.roll(ids, (ROWS - at) % ROWS, axis=1), 0.0)
    value = jnp.where((lane < HALF) & (row < 3), value, 0.0)
    value = pltpu.roll(value, to, axis=1)
    message = jnp.concatenate([chosen, value], axis=0).astype(BF16)
    for i in range(N_FAR):
        msg_ref[i] = message


def block_ids(msg_ref):
    _, q, _ = place_of()
    ids = msg_ref[:, HALF:, :].astype(F32)
    ids = ids.reshape(N_FAR // 8, 8, 8, ROWS).sum(axis=1)
    ids = jnp.concatenate([ids[i] for i in range(N_FAR // 8)], axis=1)
    lane = lax.broadcasted_iota(I32, (1, ANCHORS), 1)
    partner = (ids[0:1] * float(ROWS) + ids[1:2]).astype(I32)
    own = (lane // HALF * N_QUAD + q) * ROWS + ids[2:3].astype(I32)
    return partner, own


def column_ids(r):
    g, q, _ = place_of()
    base = (g * N_QUAD + (q ^ r)) * ROWS
    return base + lax.broadcasted_iota(I32, (ROWS, 1), 0)


def anchors_of(msg_ref):
    return jnp.concatenate([msg_ref[i, :HALF, :] for i in range(N_FAR)], axis=0)


def middle_of(anchors):
    return jnp.sum(anchors.astype(F32), axis=0, keepdims=True) * (1.0 / ANCHORS)


def block_sums(msg_ref, e0_ref, e1_ref, e2_ref, e3_ref, out_ref):
    anchors = anchors_of(msg_ref)
    partner, own = block_ids(msg_ref)
    total = jnp.zeros((1, ANCHORS), F32)
    rows = jnp.zeros((ANCHORS, 2 * EMB), F32)
    pairs = jnp.zeros((ANCHORS, EMB), F32)
    ones = jnp.ones((ROWS, EMB), BF16)
    for r, e_ref in enumerate((e0_ref, e1_ref, e2_ref, e3_ref)):
        cols_emb = e_ref[...]
        s = dot(cols_emb, anchors, ((1,), (1,)))
        cols = column_ids(r)
        positive = cols == partner
        ex = jnp.where(cols == own, 0.0, jnp.exp2(s * (INV_TEMP * LOG2E) - SHIFT * LOG2E))
        total = total + jnp.sum(ex, axis=0, keepdims=True)
        others = jnp.where(positive, 0.0, ex).astype(BF16)
        rows = rows + dot(others, jnp.concatenate([cols_emb, ones], axis=1), ((0,), (0,)))
        pairs = pairs + dot(positive.astype(F32).astype(BF16), cols_emb, ((0,), (0,)))
    rows = (rows[:, :EMB] - rows[:, EMB:] * middle_of(anchors)).astype(BF16)
    pairs = pairs.astype(BF16)
    lines = jnp.concatenate([total[:, i * ROWS : (i + 1) * ROWS] for i in range(4)], axis=0)
    high = lines.astype(BF16).astype(F32)
    lines = jnp.concatenate([high, lines - high], axis=0).astype(BF16)
    for i in range(N_FAR):
        here = slice(i * HALF, (i + 1) * HALF)
        out_ref[i, 0:16, :] = rows[here]
        out_ref[i, 16:32, :] = pairs[here]
        out_ref[i, 32:40, :] = lines


def totals_of(sums_ref):
    lines = jnp.sum(sums_ref[:, 32:40, :].astype(F32), axis=0)
    return lines[0:4] + lines[4:8]


def weights(
    msg_ref, sums_ref, e0_ref, e1_ref, e2_ref, e3_ref, keep_ref, send_ref
):
    anchors = anchors_of(msg_ref)
    partner, own = block_ids(msg_ref)
    total = totals_of(sums_ref)
    total = jnp.concatenate([total[i : i + 1] for i in range(4)], axis=1)
    offset = SHIFT * LOG2E + jnp.log2(total)
    for r, e_ref in enumerate((e0_ref, e1_ref, e2_ref, e3_ref)):
        s = dot(e_ref[...], anchors, ((1,), (1,)))
        cols = column_ids(r)
        prob = jnp.where(cols == own, 0.0, jnp.exp2(s * (INV_TEMP * LOG2E) - offset))
        w = jnp.where(cols == partner, prob - 1.0, prob).astype(BF16)
        c_ref = send_ref if r % 2 else keep_ref
        c_ref[r // 2] = dot(w, anchors, ((1,), (0,)))


def own_rows(msg_ref, sums_ref, out_ref):
    g, _, mp = place_of()
    line = lax.broadcasted_iota(I32, (4, ROWS), 0)
    total = jnp.sum(jnp.where(line == g // 8, totals_of(sums_ref), 0.0), axis=0, keepdims=True)
    total = jnp.broadcast_to(total, (HALF, ROWS))
    to = mp * HALF
    total = pltpu.roll(total, (to - (g % 8) * HALF + ROWS) % ROWS, axis=1)
    lane = lax.broadcasted_iota(I32, (HALF, ROWS), 1)
    here = lane == to + lax.broadcasted_iota(I32, (HALF, ROWS), 0)
    pair = jnp.sum(sums_ref[:, 16:32, :].astype(F32), axis=0)
    emb = msg_ref[g, 0:HALF, :].astype(F32)
    hit_of = jnp.sum(emb * pair, axis=1, keepdims=True) * INV_TEMP
    hit = jnp.sum(jnp.where(here, hit_of, 0.0), axis=0, keepdims=True)
    loss = jnp.where((lane >= to) & (lane < to + HALF), jnp.log(total) + SHIFT - hit, 0.0)
    out_ref[HALF:, :] = loss[0:8]
    total_of = jnp.sum(jnp.where(here, total, 0.0), axis=1, keepdims=True)
    ex_pair = jnp.exp(hit_of - SHIFT)
    weight = (ex_pair / total_of - 1.0).astype(BF16).astype(F32)
    rows = jnp.sum(sums_ref[:, 0:16, :].astype(F32), axis=0)
    rows = rows + (total_of - ex_pair) * middle_of(anchors_of(msg_ref))
    out_ref[0:HALF, :] = rows / total_of + weight * pair


def add_pair(window_ref, a_ref, b_ref, rows_ref, mine_ref, next_ref):
    next_ref[...] = a_ref[1] + b_ref[1]
    start = start_of(window_ref)
    rows = rows_ref[0:HALF, :]
    for at in range(0, ROWS, HALF):
        here = slice(at, at + HALF)
        mine_ref[here, :] = a_ref[0, here] + b_ref[0, here] + jnp.where(start == at, rows, 0.0)
    mine_ref[ROWS:, :] = rows_ref[HALF:, :]


def backward(
    mine_ref,
    theirs_ref,
    third_ref,
    fourth_ref,
    part_ref,
    other_ref,
    pre_ref,
    hid_ref,
    x_ref,
    w_out_ref,
    loss_ref,
    keep_ref,
    send_ref,
):
    scale = INV_TEMP / (N_FAR * N_QUAD * A_DEV)
    grad_emb = mine_ref[0:ROWS, :] + theirs_ref[0:ROWS, :]
    grad_emb = (grad_emb + (third_ref[...] + fourth_ref[...])) * scale
    loss_ref[...] = mine_ref[ROWS : ROWS + 1, 0:A_DEV] + theirs_ref[ROWS : ROWS + 1, 0:A_DEV]
    proj = part_ref[...] + other_ref[...]
    norm = norm_of(proj)
    unit = proj / norm
    inner = jnp.sum(unit * grad_emb, axis=1, keepdims=True)
    grad_proj = ((grad_emb - unit * inner) / norm).astype(BF16)
    grad_out = dot(hid_ref[...], grad_proj, ((0,), (0,)))
    grad_hidden = dot(grad_proj, w_out_ref[...], ((1,), (1,)))
    pre = pre_ref[...]
    sig = jax.nn.sigmoid(pre)
    grad_pre = (grad_hidden * sig * (1.0 + pre * (1.0 - sig))).astype(BF16)
    grad_in = dot(x_ref[...], grad_pre, ((0,), (0,)))
    bias = jnp.sum(grad_pre.astype(F32), axis=0, keepdims=True)
    first = lax.broadcasted_iota(I32, (8, 128), 0) == 0
    c = lax.axis_index("c")

    def store(half, out_ref):
        lanes = slice(half * 128, half * 128 + 128)
        for i in range(N_NEAR):
            out_ref[i, 0:32, :] = grad_in[i * 32 : i * 32 + 32, lanes]
            out_ref[i, 32:40, :] = grad_out[half * 128 + i * 8 : half * 128 + i * 8 + 8]
            line = jnp.where(first, bias[:, lanes], 0.0) if i == 0 else jnp.zeros((8, 128), F32)
            out_ref[i, 40:, :] = line

    for side in (0, 1):

        @pl.when(c == side)
        def _():
            store(side, keep_ref)
            store(1 - side, send_ref)


def add(a_ref, b_ref, out_ref):
    out_ref[...] = a_ref[...] + b_ref[...]


def sum_spread(in_ref, out_ref):
    total = jnp.sum(in_ref[...], axis=0)
    for i in range(out_ref.shape[0]):
        out_ref[i] = total


def place(side, in_ref, w_in_ref, w_out_ref, sems):
    lanes = pl.ds(pl.multiple_of(side * 128, 128), 128)
    copies = [
        pltpu.make_async_copy(in_ref.at[:, 0:32, :], w_in_ref.at[:, :, lanes], sems.at[0]),
        pltpu.make_async_copy(in_ref.at[:, 32:40, :], w_out_ref.at[side], sems.at[1]),
    ]
    for copy in copies:
        copy.start()
    return copies


def place_mine(mine_ref, loss_in_ref, w_in_ref, w_out_ref, loss_ref, sems):
    copies = place(lax.axis_index("c"), mine_ref, w_in_ref, w_out_ref, sems)
    copies.append(pltpu.make_async_copy(loss_in_ref, loss_ref, sems.at[2]))
    copies[-1].start()
    for copy in copies:
        copy.wait()


def place_theirs(
    mine_ref, theirs_ref, _, __, w_in_ref, w_out_ref, b_ref, bias_ref, sems
):
    c = lax.axis_index("c")
    copies = place(1 - c, theirs_ref, w_in_ref, w_out_ref, sems)
    own, other = mine_ref[0, 40:41, :], theirs_ref[0, 40:41, :]
    bias_ref[0:1, :] = jnp.where(c == 0, own, other)
    bias_ref[1:2, :] = jnp.where(c == 0, other, own)
    copies.append(pltpu.make_async_copy(bias_ref, b_ref, sems.at[2]))
    copies[-1].start()
    for copy in copies:
        copy.wait()


def swap(value, axes, flip):
    axes = axes if isinstance(axes, tuple) else (axes,)
    count = lax.axis_size(axes)
    return lax.ppermute(value, axes, [(i, i ^ flip) for i in range(count)])


def exchange(value, axes):
    return lax.all_to_all(value, axes, 0, 0, tiled=True)


def on_device(features, w_in, b_in, w_out, partner, window):
    line = (1, ROWS)
    part, pre, hidden, partner, window = call(
        forward,
        [((ROWS, EMB), F32), ((ROWS, 256), F32), ((ROWS, 256), BF16), (line, I32), (line, I32)],
        features,
        w_in,
        b_in.reshape(1, -1),
        w_out,
        partner.reshape(line),
        window.reshape(line),
        first=True,
    )
    other = swap(part, "mp", 1)
    emb, message = call(
        embed,
        [((ROWS, EMB), BF16), ((N_FAR, MSG, EMB), BF16)],
        window,
        part,
        other,
        partner,
    )
    anchors = exchange(message, FAR)
    blocks = [emb] + [swap(emb, QUAD, r) for r in (1, 2, 3)]
    (sums,) = call(block_sums, [((N_FAR, 40, EMB), BF16)], anchors, *blocks)
    sums = exchange(sums, FAR)
    pair = (2, ROWS, EMB)
    keep, send = call(weights, [(pair, F32), (pair, F32)], anchors, sums, *blocks)
    got = swap(send, "c", 1)
    (rows,) = call(own_rows, [((HALF + 8, EMB), F32)], anchors, sums)
    mine, away = call(
        add_pair,
        [((ROWS + 8, EMB), F32), ((ROWS, EMB), F32)],
        window,
        keep,
        got,
        rows,
    )
    fourth = swap(away, ("yh", "mp"), 3)
    third = swap(away, "yh", 1)
    theirs = swap(mine, "mp", 1)
    half = (N_NEAR, PART, EMB)
    row_loss, keep, send = call(
        backward,
        [((1, A_DEV), F32), (half, F32), (half, F32)],
        mine,
        theirs,
        third,
        fourth,
        part,
        other,
        pre,
        hidden,
        features,
        w_out,
    )
    got = swap(send, "c", 1)
    (both,) = call(add, [(half, F32)], keep, got)
    (both,) = call(sum_spread, [((4, PART, EMB), F32)], exchange(both, NEAR))
    (both,) = call(sum_spread, [(half, F32)], exchange(both, "zh"))
    both = exchange(both, NEAR)
    got = swap(both, "c", 1)
    whole = [((N_NEAR, 32, 256), F32), ((2, N_NEAR, 8, EMB), F32)]
    sems = [pltpu.SemaphoreType.DMA((3,))]
    *grads, row_loss = call(
        place_mine,
        whole + [((1, A_DEV), F32)],
        both,
        row_loss,
        scratch=sems,
        last=(0, 1, 2),
    )
    grad_in, grad_out, grad_b = call(
        place_theirs,
        whole + [((2, 128), F32)],
        both,
        got,
        *grads,
        scratch=[pltpu.VMEM((2, 128), F32)] + sems,
        last=(0, 1, 2),
        alias={2: 0, 3: 1},
    )
    return (
        row_loss.reshape(-1),
        grad_in.reshape(512, 256),
        grad_b.reshape(-1),
        grad_out.reshape(256, EMB),
    )


def solution(mesh):
    finer = Mesh(mesh.devices.reshape(*SIZES.values(), mesh.shape["mp"]), (*SIZES, "mp"))
    placed = (P(DP, None), P(None, "mp"), P("mp"), P("mp", None), P(DP), P())
    return jax.shard_map(
        on_device,
        mesh=finer,
        in_specs=placed,
        out_specs=(P(DP), P(None, "mp"), P("mp"), P("mp", None)),
        check_vma=False,
    )
```

```python
import jax
import jax.numpy as jnp
from jax import lax
from jax.experimental import pallas as pl
from jax.experimental.pallas import tpu as pltpu
from jax.sharding import Mesh
from jax.sharding import PartitionSpec as P


SIZES = {"zh": 4, "zl": 2, "x": 4, "yh": 2, "c": 2}
DP = ("zh", "zl", "x", "yh", "c")
NEAR = ("yh", "x", "zl")
FAR = ("x", "zh", "zl")
QUAD = ("yh", "c")

ROWS = 128
A_DEV = 32
HALF = 16
EMB = 128
N_FAR = 32
N_QUAD = 4
ANCHORS = N_FAR * HALF
MSG = 24
PART = 48
N_NEAR = 16

INV_TEMP = 10.0
SHIFT = 10.0
EPS = 1e-06
LOG2E = 1.4426950408889634
BF16 = jnp.bfloat16
F32 = jnp.float32
I32 = jnp.int32


def call(kernel, outs, *args, scratch=(), first=False, last=(), alias={}):
    specs = [
        pl.BlockSpec(memory_space=pl.ANY if i in alias else pltpu.VMEM) for i in range(len(args))
    ]
    if not first:
        args = [
            a if i in alias else pltpu.with_memory_space_constraint(a, pltpu.VMEM)
            for i, a in enumerate(args)
        ]
    shapes = [jax.ShapeDtypeStruct(s, d) if last else pltpu.VMEM(s, d) for s, d in outs]
    return pl.pallas_call(
        kernel,
        out_shape=shapes,
        in_specs=specs,
        out_specs=[
            pl.BlockSpec(memory_space=pl.ANY if i in last else pltpu.VMEM) for i in range(len(outs))
        ],
        scratch_shapes=list(scratch),
        input_output_aliases=alias,
    )(*args)


def place_of():
    return lax.axis_index(FAR), lax.axis_index(QUAD), lax.axis_index("mp")


def quad_of(far):
    return far % 8 * 4 + far // 8


def start_of(window_ref):
    g, q, mp = place_of()
    lane = lax.broadcasted_iota(I32, (1, ROWS), 1)
    block = jnp.where(lane == quad_of(g) * N_QUAD + q, window_ref[...], 0)
    return jnp.sum(block, axis=1, keepdims=True) * A_DEV + mp * HALF


def dot(a, b, dims):
    return lax.dot_general(a, b, (dims, ((), ())), preferred_element_type=F32)


def forward(
    x_ref, w_in_ref, b_ref, w_out_ref, *refs
):
    partner_ref, window_ref, part_ref, pre_ref, hid_ref, partner_out_ref, window_out_ref = refs
    partner_out_ref[...] = partner_ref[...]
    window_out_ref[...] = window_ref[...]
    pre = dot(x_ref[...], w_in_ref[...], ((1,), (0,))) + b_ref[...]
    hidden = (pre * jax.nn.sigmoid(pre)).astype(BF16)
    pre_ref[...] = pre
    hid_ref[...] = hidden
    part_ref[...] = dot(hidden, w_out_ref[...], ((1,), (0,)))


def norm_of(proj):
    return jnp.sqrt(jnp.sum(proj * proj, axis=1, keepdims=True) + EPS)


def embed(window_ref, part_ref, other_ref, partner_ref, emb_ref, msg_ref):
    g, _, _ = place_of()
    proj = part_ref[...] + other_ref[...]
    rounded = (proj / norm_of(proj)).astype(BF16)
    emb_ref[...] = rounded
    emb = rounded.astype(F32)
    start = start_of(window_ref)
    to = (g % 8) * HALF
    lane = lax.broadcasted_iota(I32, (8, ROWS), 1)
    row = lax.broadcasted_iota(I32, (8, ROWS), 0)
    partner = jnp.broadcast_to(partner_ref[...], (8, ROWS))
    ids = jnp.where(
        row == 0, partner // ROWS, jnp.where(row == 1, partner % ROWS, lane)
    ).astype(F32)
    chosen = jnp.zeros((HALF, EMB), F32)
    value = jnp.zeros((8, ROWS), F32)
    for at in range(0, ROWS, HALF):
        chosen = chosen + jnp.where(start == at, emb[at : at + HALF], 0.0)
        value = value + jnp.where(start == at, pltpu.roll(ids, (ROWS - at) % ROWS, axis=1), 0.0)
    value = jnp.where((lane < HALF) & (row < 3), value, 0.0)
    value = pltpu.roll(value, to, axis=1)
    message = jnp.concatenate([chosen, value], axis=0).astype(BF16)
    for i in range(N_FAR):
        msg_ref[i] = message


def block_ids(msg_ref):
    _, q, _ = place_of()
    ids = msg_ref[:, HALF:, :].astype(F32)
    ids = ids.reshape(N_FAR // 8, 8, 8, ROWS).sum(axis=1)
    ids = jnp.concatenate([ids[i] for i in range(N_FAR // 8)], axis=1)
    lane = lax.broadcasted_iota(I32, (1, ANCHORS), 1)
    partner = (ids[0:1] * float(ROWS) + ids[1:2]).astype(I32)
    own = (quad_of(lane // HALF) * N_QUAD + q) * ROWS + ids[2:3].astype(I32)
    return partner, own


def column_ids(r):
    g, q, _ = place_of()
    base = (quad_of(g) * N_QUAD + (q ^ r)) * ROWS
    return base + lax.broadcasted_iota(I32, (ROWS, 1), 0)


def anchors_of(msg_ref):
    return jnp.concatenate([msg_ref[i, :HALF, :] for i in range(N_FAR)], axis=0)


def middle_of(anchors):
    return jnp.sum(anchors.astype(F32), axis=0, keepdims=True) * (1.0 / ANCHORS)


def block_sums(msg_ref, e0_ref, e1_ref, e2_ref, e3_ref, out_ref):
    anchors = anchors_of(msg_ref)
    partner, own = block_ids(msg_ref)
    total = jnp.zeros((1, ANCHORS), F32)
    rows = jnp.zeros((ANCHORS, 2 * EMB), F32)
    pairs = jnp.zeros((ANCHORS, EMB), F32)
    ones = jnp.ones((ROWS, EMB), BF16)
    for r, e_ref in enumerate((e0_ref, e1_ref, e2_ref, e3_ref)):
        cols_emb = e_ref[...]
        s = dot(cols_emb, anchors, ((1,), (1,)))
        cols = column_ids(r)
        positive = cols == partner
        ex = jnp.where(cols == own, 0.0, jnp.exp2(s * (INV_TEMP * LOG2E) - SHIFT * LOG2E))
        total = total + jnp.sum(ex, axis=0, keepdims=True)
        others = jnp.where(positive, 0.0, ex).astype(BF16)
        rows = rows + dot(others, jnp.concatenate([cols_emb, ones], axis=1), ((0,), (0,)))
        pairs = pairs + dot(positive.astype(F32).astype(BF16), cols_emb, ((0,), (0,)))
    rows = (rows[:, :EMB] - rows[:, EMB:] * middle_of(anchors)).astype(BF16)
    pairs = pairs.astype(BF16)
    lines = jnp.concatenate([total[:, i * ROWS : (i + 1) * ROWS] for i in range(4)], axis=0)
    high = lines.astype(BF16).astype(F32)
    lines = jnp.concatenate([high, lines - high], axis=0).astype(BF16)
    for i in range(N_FAR):
        here = slice(i * HALF, (i + 1) * HALF)
        out_ref[i, 0:16, :] = rows[here]
        out_ref[i, 16:32, :] = pairs[here]
        out_ref[i, 32:40, :] = lines


def totals_of(sums_ref):
    lines = jnp.sum(sums_ref[:, 32:40, :].astype(F32), axis=0)
    return lines[0:4] + lines[4:8]


def weights(
    msg_ref, sums_ref, e0_ref, e1_ref, e2_ref, e3_ref, keep_ref, send_ref
):
    anchors = anchors_of(msg_ref)
    partner, own = block_ids(msg_ref)
    total = totals_of(sums_ref)
    total = jnp.concatenate([total[i : i + 1] for i in range(4)], axis=1)
    offset = SHIFT * LOG2E + jnp.log2(total)
    for r, e_ref in enumerate((e0_ref, e1_ref, e2_ref, e3_ref)):
        s = dot(e_ref[...], anchors, ((1,), (1,)))
        cols = column_ids(r)
        prob = jnp.where(cols == own, 0.0, jnp.exp2(s * (INV_TEMP * LOG2E) - offset))
        w = jnp.where(cols == partner, prob - 1.0, prob).astype(BF16)
        c_ref = send_ref if r % 2 else keep_ref
        c_ref[r // 2] = dot(w, anchors, ((1,), (0,)))


def own_rows(msg_ref, sums_ref, out_ref):
    g, _, mp = place_of()
    line = lax.broadcasted_iota(I32, (4, ROWS), 0)
    total = jnp.sum(jnp.where(line == g // 8, totals_of(sums_ref), 0.0), axis=0, keepdims=True)
    total = jnp.broadcast_to(total, (HALF, ROWS))
    to = mp * HALF
    total = pltpu.roll(total, (to - (g % 8) * HALF + ROWS) % ROWS, axis=1)
    lane = lax.broadcasted_iota(I32, (HALF, ROWS), 1)
    here = lane == to + lax.broadcasted_iota(I32, (HALF, ROWS), 0)
    pair = jnp.sum(sums_ref[:, 16:32, :].astype(F32), axis=0)
    emb = msg_ref[g, 0:HALF, :].astype(F32)
    hit_of = jnp.sum(emb * pair, axis=1, keepdims=True) * INV_TEMP
    hit = jnp.sum(jnp.where(here, hit_of, 0.0), axis=0, keepdims=True)
    loss = jnp.where((lane >= to) & (lane < to + HALF), jnp.log(total) + SHIFT - hit, 0.0)
    out_ref[HALF:, :] = loss[0:8]
    total_of = jnp.sum(jnp.where(here, total, 0.0), axis=1, keepdims=True)
    ex_pair = jnp.exp(hit_of - SHIFT)
    weight = (ex_pair / total_of - 1.0).astype(BF16).astype(F32)
    rows = jnp.sum(sums_ref[:, 0:16, :].astype(F32), axis=0)
    rows = rows + (total_of - ex_pair) * middle_of(anchors_of(msg_ref))
    out_ref[0:HALF, :] = rows / total_of + weight * pair


def add_pair(window_ref, a_ref, b_ref, rows_ref, mine_ref, next_ref):
    next_ref[...] = a_ref[1] + b_ref[1]
    start = start_of(window_ref)
    rows = rows_ref[0:HALF, :]
    for at in range(0, ROWS, HALF):
        here = slice(at, at + HALF)
        mine_ref[here, :] = a_ref[0, here] + b_ref[0, here] + jnp.where(start == at, rows, 0.0)
    mine_ref[ROWS:, :] = rows_ref[HALF:, :]


def backward(
    mine_ref,
    theirs_ref,
    third_ref,
    fourth_ref,
    part_ref,
    other_ref,
    pre_ref,
    hid_ref,
    x_ref,
    w_out_ref,
    loss_ref,
    keep_ref,
    send_ref,
):
    scale = INV_TEMP / (N_FAR * N_QUAD * A_DEV)
    grad_emb = mine_ref[0:ROWS, :] + theirs_ref[0:ROWS, :]
    grad_emb = (grad_emb + (third_ref[...] + fourth_ref[...])) * scale
    loss_ref[...] = mine_ref[ROWS : ROWS + 1, 0:A_DEV] + theirs_ref[ROWS : ROWS + 1, 0:A_DEV]
    proj = part_ref[...] + other_ref[...]
    norm = norm_of(proj)
    unit = proj / norm
    inner = jnp.sum(unit * grad_emb, axis=1, keepdims=True)
    grad_proj = ((grad_emb - unit * inner) / norm).astype(BF16)
    grad_out = dot(hid_ref[...], grad_proj, ((0,), (0,)))
    grad_hidden = dot(grad_proj, w_out_ref[...], ((1,), (1,)))
    pre = pre_ref[...]
    sig = jax.nn.sigmoid(pre)
    grad_pre = (grad_hidden * sig * (1.0 + pre * (1.0 - sig))).astype(BF16)
    grad_in = dot(x_ref[...], grad_pre, ((0,), (0,)))
    bias = jnp.sum(grad_pre.astype(F32), axis=0, keepdims=True)
    first = lax.broadcasted_iota(I32, (8, 128), 0) == 0
    c = lax.axis_index("c")

    def store(half, out_ref):
        lanes = slice(half * 128, half * 128 + 128)
        for i in range(N_NEAR):
            out_ref[i, 0:32, :] = grad_in[i * 32 : i * 32 + 32, lanes]
            out_ref[i, 32:40, :] = grad_out[half * 128 + i * 8 : half * 128 + i * 8 + 8]
            line = jnp.where(first, bias[:, lanes], 0.0) if i == 0 else jnp.zeros((8, 128), F32)
            out_ref[i, 40:, :] = line

    for side in (0, 1):

        @pl.when(c == side)
        def _():
            store(side, keep_ref)
            store(1 - side, send_ref)


def add(a_ref, b_ref, out_ref):
    out_ref[...] = a_ref[...] + b_ref[...]


def sum_spread(in_ref, out_ref):
    total = jnp.sum(in_ref[...], axis=0)
    for i in range(out_ref.shape[0]):
        out_ref[i] = total


def place(side, in_ref, w_in_ref, w_out_ref, sems):
    lanes = pl.ds(pl.multiple_of(side * 128, 128), 128)
    copies = [
        pltpu.make_async_copy(in_ref.at[:, 0:32, :], w_in_ref.at[:, :, lanes], sems.at[0]),
        pltpu.make_async_copy(in_ref.at[:, 32:40, :], w_out_ref.at[side], sems.at[1]),
    ]
    for copy in copies:
        copy.start()
    return copies


def place_mine(mine_ref, loss_in_ref, w_in_ref, w_out_ref, loss_ref, sems):
    copies = place(lax.axis_index("c"), mine_ref, w_in_ref, w_out_ref, sems)
    copies.append(pltpu.make_async_copy(loss_in_ref, loss_ref, sems.at[2]))
    copies[-1].start()
    for copy in copies:
        copy.wait()


def place_theirs(
    mine_ref, theirs_ref, _, __, w_in_ref, w_out_ref, b_ref, bias_ref, sems
):
    c = lax.axis_index("c")
    copies = place(1 - c, theirs_ref, w_in_ref, w_out_ref, sems)
    own, other = mine_ref[0, 40:41, :], theirs_ref[0, 40:41, :]
    bias_ref[0:1, :] = jnp.where(c == 0, own, other)
    bias_ref[1:2, :] = jnp.where(c == 0, other, own)
    copies.append(pltpu.make_async_copy(bias_ref, b_ref, sems.at[2]))
    copies[-1].start()
    for copy in copies:
        copy.wait()


def swap(value, axes, flip):
    axes = axes if isinstance(axes, tuple) else (axes,)
    count = lax.axis_size(axes)
    return lax.ppermute(value, axes, [(i, i ^ flip) for i in range(count)])


def exchange(value, axes):
    return lax.all_to_all(value, axes, 0, 0, tiled=True)


def on_device(features, w_in, b_in, w_out, partner, window):
    line = (1, ROWS)
    part, pre, hidden, partner, window = call(
        forward,
        [((ROWS, EMB), F32), ((ROWS, 256), F32), ((ROWS, 256), BF16), (line, I32), (line, I32)],
        features,
        w_in,
        b_in.reshape(1, -1),
        w_out,
        partner.reshape(line),
        window.reshape(line),
        first=True,
    )
    other = swap(part, "mp", 1)
    emb, message = call(
        embed,
        [((ROWS, EMB), BF16), ((N_FAR, MSG, EMB), BF16)],
        window,
        part,
        other,
        partner,
    )
    anchors = exchange(message, FAR)
    blocks = [emb] + [swap(emb, QUAD, r) for r in (1, 2, 3)]
    (sums,) = call(block_sums, [((N_FAR, 40, EMB), BF16)], anchors, *blocks)
    sums = exchange(sums, FAR)
    pair = (2, ROWS, EMB)
    keep, send = call(weights, [(pair, F32), (pair, F32)], anchors, sums, *blocks)
    got = swap(send, "c", 1)
    (rows,) = call(own_rows, [((HALF + 8, EMB), F32)], anchors, sums)
    mine, away = call(
        add_pair,
        [((ROWS + 8, EMB), F32), ((ROWS, EMB), F32)],
        window,
        keep,
        got,
        rows,
    )
    fourth = swap(away, ("yh", "mp"), 3)
    third = swap(away, "yh", 1)
    theirs = swap(mine, "mp", 1)
    half = (N_NEAR, PART, EMB)
    row_loss, keep, send = call(
        backward,
        [((1, A_DEV), F32), (half, F32), (half, F32)],
        mine,
        theirs,
        third,
        fourth,
        part,
        other,
        pre,
        hidden,
        features,
        w_out,
    )
    got = swap(send, "c", 1)
    (both,) = call(add, [(half, F32)], keep, got)
    (both,) = call(sum_spread, [((4, PART, EMB), F32)], exchange(both, NEAR))
    (both,) = call(sum_spread, [(half, F32)], exchange(both, "zh"))
    both = exchange(both, NEAR)
    got = swap(both, "c", 1)
    whole = [((N_NEAR, 32, 256), F32), ((2, N_NEAR, 8, EMB), F32)]
    sems = [pltpu.SemaphoreType.DMA((3,))]
    *grads, row_loss = call(
        place_mine,
        whole + [((1, A_DEV), F32)],
        both,
        row_loss,
        scratch=sems,
        last=(0, 1, 2),
    )
    grad_in, grad_out, grad_b = call(
        place_theirs,
        whole + [((2, 128), F32)],
        both,
        got,
        *grads,
        scratch=[pltpu.VMEM((2, 128), F32)] + sems,
        last=(0, 1, 2),
        alias={2: 0, 3: 1},
    )
    return (
        row_loss.reshape(-1),
        grad_in.reshape(512, 256),
        grad_b.reshape(-1),
        grad_out.reshape(256, EMB),
    )


def solution(mesh):
    finer = Mesh(mesh.devices.reshape(*SIZES.values(), mesh.shape["mp"]), (*SIZES, "mp"))
    placed = (P(DP, None), P(None, "mp"), P("mp"), P("mp", None), P(DP), P())
    return jax.shard_map(
        on_device,
        mesh=finer,
        in_specs=placed,
        out_specs=(P(DP), P(None, "mp"), P("mp"), P("mp", None)),
        check_vma=False,
    )
```
